256 devices in a mesh: sens: 16 (over y, x), pts: 16 (over z, core).
Axes of the slice: x: 4, y: 4, z: 8, core: 2. Of those that a mesh axis runs over, the one named last changes fastest.
Arguments:
- records: float32 [4, 640, 383], P(None, 'sens'), may hold values from -8 to 8
- tiles: bfloat16 [2, 640, 1024, 384], P(None, 'sens', 'pts'), may hold values from -6 to 6
- gauge_response_blocks: bfloat16 [2, 64, 1024, 384], P(None, 'sens', 'pts'), may hold values from -6 to 6
- prior: float32 [1024, 384], P('pts'), may hold values from 0.1 to 1
- noise: float32 [640], P('sens'), may hold values from 0.2 to 1
Outputs:
- krylov_estimate: float32 [4, 640, 383], P(None, 'sens')
- predicted_wave_records: float32 [4, 64, 383], P(None, 'sens')
The draws below stay inside these ranges and needn't reach their ends.
All inputs are finite; a program needn't handle non-finite values.
Results may differ from the reference program's by a relative error of at most 0.0059.
Values may be sent and summed in bfloat16 or wider, within the bound.
No kernel may reach another device: no remote copies, remote signals or barrier semaphores. Data moves between devices by JAX's collectives and lax.ppermute only.
A program may use at most 128 MiB of HBM per device.

```python
import math
import jax
import jax.numpy as jnp
from jax import lax

REALS = 4
SENSORS = 640
SEAFLOOR_COUNT = 1024
SITE_COUNT = 64
STEPS = 383
ITERS = 2
PADDED = 766
FREQUENCY_COUNT = 384


def draw_records(key, part):
    first, second, third = jax.random.split(key, 3)
    shape = (REALS, SENSORS, STEPS)
    ramp = jnp.exp(math.log(3.0) * jnp.arange(SENSORS, dtype=jnp.float32) / max(SENSORS - 1, 1))
    realm = jnp.exp(jax.random.uniform(third, (REALS, 1, 1), jnp.float32, math.log(0.5), math.log(2.0)))
    base = jax.random.normal(first, shape, jnp.float32)
    rough = jnp.exp(jax.random.uniform(second, (SENSORS,), jnp.float32, 0.0, math.log(3.0)))
    values = base * (ramp * rough)[None, :, None] * realm / 4.0
    return jnp.clip(values, -8.0, 8.0)


def block_levels(rng, dims, cuts, smallest, high):
    def one(axis_at, shards_of):
        draws = jax.random.uniform(jax.random.fold_in(jax.random.fold_in(rng, 6), axis_at), (shards_of,), jnp.float32, smallest / len(cuts), high / len(cuts))
        return jnp.repeat(jnp.exp(draws), dims[axis_at] // shards_of).reshape((-1,) + (1,) * (len(dims) - axis_at - 1))

    loudness = one(*cuts[0])
    for cut in cuts[1:]:
        loudness = loudness * one(*cut)
    return loudness


def gaussian(key, dims, scale, most, cuts=(), held_as=jnp.bfloat16):
    factor_of = block_levels(key, dims, cuts, -0.22, 0.18) if cuts else 1.0
    result = jax.random.normal(key, dims, jnp.float32) * scale * factor_of
    return jnp.minimum(jnp.maximum(result, -most), most).astype(held_as)


def setup_inputs(seed: int = 0) -> dict:
    splits = jax.random.split(jax.random.key(seed), 6)
    return {
        "records": draw_records(jax.random.fold_in(splits[5], 71), 0),
        "tiles": gaussian(splits[1], (2, SENSORS, SEAFLOOR_COUNT, FREQUENCY_COUNT), 1.0, 6.0, ((1, 16), (2, 16))),
        "gauge_response_blocks": gaussian(splits[2], (2, SITE_COUNT, SEAFLOOR_COUNT, FREQUENCY_COUNT), 1.0, 6.0, ((1, 16), (2, 16))),
        "prior": jnp.clip(jnp.exp(math.log(1.0) - 2.3025851 * jax.random.uniform(splits[3], (SEAFLOOR_COUNT, FREQUENCY_COUNT), jnp.float32) ** block_levels(splits[3], (SEAFLOOR_COUNT, FREQUENCY_COUNT), ((0, 16),), -0.2, 0.2)), 0.1, 1.0),
        "noise": jnp.clip(jnp.exp(math.log(1.0) - 1.609438 * jax.random.uniform(splits[4], (SENSORS,), jnp.float32) ** block_levels(splits[4], (SENSORS,), ((0, 16),), -0.2, 0.2)), 0.2, 1.0),
    }


def tables():
    times = jnp.arange(STEPS, dtype=jnp.int32)
    freqs = jnp.arange(FREQUENCY_COUNT, dtype=jnp.int32)
    phase = (times[:, None] * freqs[None, :]) % PADDED
    angle = phase.astype(jnp.float32) * (2.0 * math.pi / PADDED)
    edge = (freqs == 0) | (freqs == PADDED // 2)
    weights = jnp.where(edge, 1.0, 2.0).astype(jnp.float32) / PADDED
    return jnp.cos(angle) * weights[None, :], jnp.sin(angle) * weights[None, :]


def analyze(series, even_harmonic_term, odd_harmonic_term):
    real_part = jnp.einsum('bst,tf->bsf', series, even_harmonic_term, precision=lax.Precision.HIGHEST)
    imaginary_part = -jnp.einsum('bst,tf->bsf', series, odd_harmonic_term, precision=lax.Precision.HIGHEST)
    return jnp.stack([real_part, imaginary_part]).astype(jnp.bfloat16)


def synthesize(real_part, imaginary_part, even_harmonic_term, odd_harmonic_term):
    first = jnp.einsum('bsf,tf->bst', real_part, even_harmonic_term, precision=lax.Precision.HIGHEST)
    second = jnp.einsum('bsf,tf->bst', imaginary_part, odd_harmonic_term, precision=lax.Precision.HIGHEST)
    return first - second


def adjoint(spectra, tiles):
    def single(index):
        spec = lax.dynamic_index_in_dim(spectra, index, 3, keepdims=False)
        tile = lax.dynamic_index_in_dim(tiles, index, 3, keepdims=False)
        real_part = jnp.dot(spec[0], tile[0], preferred_element_type=jnp.float32) + jnp.dot(spec[1], tile[1], preferred_element_type=jnp.float32)
        imaginary_part = jnp.dot(spec[1], tile[0], preferred_element_type=jnp.float32) - jnp.dot(spec[0], tile[1], preferred_element_type=jnp.float32)
        return jnp.stack([real_part, imaginary_part])
    indices = jnp.arange(FREQUENCY_COUNT, dtype=jnp.int32)
    out = lax.map(single, indices)
    return jnp.moveaxis(out, 0, 3)


def forward_apply(weighted, tiles):
    def single(index):
        point = lax.dynamic_index_in_dim(weighted, index, 3, keepdims=False)
        tile = lax.dynamic_index_in_dim(tiles, index, 3, keepdims=False)
        real_part = jnp.dot(point[0], tile[0].T, preferred_element_type=jnp.float32) - jnp.dot(point[1], tile[1].T, preferred_element_type=jnp.float32)
        imaginary_part = jnp.dot(point[0], tile[1].T, preferred_element_type=jnp.float32) + jnp.dot(point[1], tile[0].T, preferred_element_type=jnp.float32)
        return jnp.stack([real_part, imaginary_part])
    indices = jnp.arange(FREQUENCY_COUNT, dtype=jnp.int32)
    out = jnp.moveaxis(lax.map(single, indices), 0, 3)
    return out[0], out[1]


def weigh(series, tiles, prior, even_harmonic_term, odd_harmonic_term):
    points = adjoint(analyze(series, even_harmonic_term, odd_harmonic_term), tiles)
    return (points * prior[None, None, :, :]).astype(jnp.bfloat16)


def reference(records, tiles, gauge_response_blocks, prior, noise):
    even_harmonic_term, odd_harmonic_term = tables()

    def covariance(series):
        weighted = weigh(series, tiles, prior, even_harmonic_term, odd_harmonic_term)
        real_part, imaginary_part = forward_apply(weighted, tiles)
        return synthesize(real_part, imaginary_part, even_harmonic_term, odd_harmonic_term) + noise[None, :, None] * series

    krylov_estimate = jnp.zeros_like(records)
    residual = records
    direction = records
    norm_now = jnp.sum(residual * residual, axis=(1, 2))
    for step in range(ITERS):
        image = covariance(direction)
        alpha = norm_now / jnp.sum(direction * image, axis=(1, 2))
        krylov_estimate = krylov_estimate + alpha[:, None, None] * direction
        residual = residual - alpha[:, None, None] * image
        norm_next = jnp.sum(residual * residual, axis=(1, 2))
        direction = residual + (norm_next / norm_now)[:, None, None] * direction
        norm_now = norm_next
    weighted = weigh(krylov_estimate, tiles, prior, even_harmonic_term, odd_harmonic_term)
    real_part, imaginary_part = forward_apply(weighted, gauge_response_blocks)
    return krylov_estimate, synthesize(real_part, imaginary_part, even_harmonic_term, odd_harmonic_term)
```

```python
import math

import jax
import jax.numpy as jnp
from jax import lax
from jax.sharding import Mesh
from jax.sharding import PartitionSpec as P

SENS = ("y", "x")
PTS = ("z", "core")
HIGH = lax.Precision.HIGHEST


def tables(steps, freqs_count, padded):
    times = jnp.arange(steps, dtype=jnp.int32)
    freqs = jnp.arange(freqs_count, dtype=jnp.int32)
    phase = times[:, None] * freqs[None, :] % padded
    angle = phase.astype(jnp.float32) * (2.0 * math.pi / padded)
    edge = (freqs == 0) | (freqs == padded // 2)
    weights = jnp.where(edge, 1.0, 2.0).astype(jnp.float32) / padded
    return (jnp.cos(angle) * weights[None, :], jnp.sin(angle) * weights[None, :])


def split(values):
    high = lax.reduce_precision(values, 8, 7)
    rest = values - high
    middle = lax.reduce_precision(rest, 8, 7)
    return jnp.stack([high, middle, rest - middle])


def scalar_rows(values, rows, columns):
    pieces = split(values).reshape(1, -1)
    return jnp.pad(pieces, ((0, rows - 1), (0, columns - pieces.shape[1]))).astype(jnp.bfloat16)


def read_scalars(block, count, reals):
    pieces = block[:, 0, : 3 * count * reals].astype(jnp.float32)
    return jnp.sum(pieces.reshape(-1, 3, count, reals), axis=(0, 1))


def to_all(block, axes, size):
    return lax.all_to_all(jnp.broadcast_to(block[None], (size,) + block.shape), axes, 0, 0)


def analyze(series, cosine, sine):
    real_part = jnp.einsum("bst,tf->bsf", series, cosine, precision=HIGH)
    imaginary_part = -jnp.einsum("bst,tf->bsf", series, sine, precision=HIGH)
    return jnp.stack([real_part, imaginary_part]).astype(jnp.bfloat16)


def adjoint_local(spectra, tiles):
    real_part = jnp.einsum("cbsf,cspf->bpf", spectra, tiles, preferred_element_type=jnp.float32)
    swapped = jnp.stack([spectra[1], -spectra[0]])
    imaginary_part = jnp.einsum(
        "cbsf,cspf->bpf", swapped, tiles, preferred_element_type=jnp.float32
    )
    return jnp.stack([real_part, imaginary_part])


def forward_local(weighted, tiles, cosine, sine):
    first_pair = jnp.stack([weighted[0], -weighted[1]])
    second_pair = jnp.stack([weighted[1], weighted[0]])
    real_part = jnp.einsum("cbpf,crpf->brf", first_pair, tiles, preferred_element_type=jnp.float32)
    imaginary_part = jnp.einsum(
        "cbpf,crpf->brf", second_pair, tiles, preferred_element_type=jnp.float32
    )
    first = jnp.einsum("brf,tf->brt", real_part, cosine, precision=HIGH)
    return first - jnp.einsum("brf,tf->brt", imaginary_part, sine, precision=HIGH)


def on_device(records, tiles, gauges, prior, noise):
    reals, sensors, steps = records.shape
    points, freqs = prior.shape
    sites = gauges.shape[1]
    cosine, sine = tables(steps, freqs, 2 * steps)
    senders = lax.axis_size("y") * lax.axis_size("x")
    heights = lax.axis_size("z")
    place = lax.axis_index("y") * lax.axis_size("x") + lax.axis_index("x")
    core = lax.axis_index("core")
    chunk = 2 * reals * points // senders
    start = lax.rem(place * chunk, points)
    prior_chunk = lax.dynamic_slice(prior, (start, 0), (chunk, freqs))
    noisy = noise[None, :, None]

    def swap(block):
        return lax.ppermute(block, "core", [(0, 1), (1, 0)])

    def point_sum(series, scalars):
        partial_points = adjoint_local(analyze(series, cosine, sine), tiles)
        block = partial_points.reshape(senders, chunk, freqs).astype(jnp.bfloat16)
        extra = scalar_rows(scalars, 16, freqs)
        extra = jnp.broadcast_to(extra[None], (senders, 16, freqs))
        got = lax.all_to_all(jnp.concatenate([block, extra], axis=1), SENS, 0, 0)
        total = jnp.sum(got[:, :chunk].astype(jnp.float32), axis=0)
        return total, read_scalars(got[:, chunk:], scalars.shape[0], reals)

    def weigh(total):
        weighted = to_all((total * prior_chunk).astype(jnp.bfloat16), SENS, senders)
        weighted = weighted.reshape(2, reals, points, freqs)
        wide = weighted.astype(jnp.float32)
        return weighted, jnp.sum(wide * wide / prior[None, None], axis=(0, 2, 3))

    def squares(first, second):
        return jnp.sum(first * second, axis=(1, 2))

    begin = jnp.stack([squares(records, records), squares(records, records * noisy)])
    points_0, (norm_0, noise_0) = point_sum(records, begin)
    weighted_0, energy_0 = weigh(points_0)
    image = forward_local(weighted_0, tiles, cosine, sine).reshape(reals * sensors, steps)
    image = jnp.pad(image, ((0, 0), (0, freqs - steps)))
    half = reals * sensors // 2
    mine = lax.dynamic_slice(image, (core * half, 0), (half, freqs))
    other = lax.dynamic_slice(image, ((1 - core) * half, 0), (half, freqs))
    sent = jnp.concatenate([other, jnp.pad(energy_0[None], ((0, 7), (0, freqs - reals)))])
    got = swap(sent)
    pair = mine + got[:half]
    energy_pair = energy_0 + got[half, :reals]
    block = jnp.concatenate([pair.astype(jnp.bfloat16), scalar_rows(energy_pair[None], 16, freqs)])
    got = to_all(block, "z", heights)
    mine = jnp.sum(got[:, :half].astype(jnp.float32), axis=0)
    energy_0 = read_scalars(got[:, half:], 1, reals)[0]
    theirs = swap(mine)
    image = jnp.where(core == 0, jnp.concatenate([mine, theirs]), jnp.concatenate([theirs, mine]))
    image = image[:, :steps].reshape(reals, sensors, steps) + noisy * records
    alpha_0 = norm_0 / (energy_0 + noise_0)
    residual = records - alpha_0[:, None, None] * image

    begin = jnp.stack(
        [
            squares(residual, residual),
            squares(residual, residual * noisy),
            squares(residual, records * noisy),
        ]
    )
    points_1, (norm_1, noise_1, noise_01) = point_sum(residual, begin)
    beta = norm_1 / norm_0
    mine_beta = lax.dynamic_index_in_dim(beta, lax.rem(place * chunk // points, reals), 0)
    points_1 = points_1 + mine_beta * points_0
    weighted_1, energy_1 = weigh(points_1)
    site_0 = forward_local(weighted_0, gauges, cosine, sine)
    site_1 = forward_local(weighted_1, gauges, cosine, sine)
    block = jnp.stack([site_0, site_1]).reshape(2 * reals * sites, steps)
    block = jnp.pad(block, ((0, 0), (0, freqs - steps)))
    block = jnp.concatenate([block, jnp.pad(energy_1[None], ((0, 7), (0, freqs - reals)))])
    block = block + swap(block)
    rows = 2 * reals * sites
    block = jnp.concatenate(
        [block[:rows].astype(jnp.bfloat16), scalar_rows(block[rows : rows + 1, :reals], 16, freqs)]
    )
    got = to_all(block, "z", heights)
    site_0, site_1 = jnp.sum(got[:, :rows, :steps].astype(jnp.float32), axis=0).reshape(
        2, reals, sites, steps
    )
    energy_1 = read_scalars(got[:, rows:], 1, reals)[0]
    curve = energy_1 + noise_1 + 2.0 * beta * noise_01 + beta * beta * noise_0
    alpha_1 = norm_1 / curve
    direction = residual + beta[:, None, None] * records
    estimate = alpha_0[:, None, None] * records + alpha_1[:, None, None] * direction
    predicted = alpha_0[:, None, None] * site_0 + alpha_1[:, None, None] * site_1
    return (estimate, predicted)


def solution(mesh):
    fine = Mesh(mesh.devices.reshape(4, 4, 8, 2), SENS + PTS)
    return jax.shard_map(
        on_device,
        mesh=fine,
        in_specs=(
            P(None, SENS, None),
            P(None, SENS, PTS, None),
            P(None, SENS, PTS, None),
            P(PTS, None),
            P(SENS),
        ),
        out_specs=(P(None, SENS, None), P(None, SENS, None)),
        check_vma=False,
    )
```

```python
import functools
import math

import jax
import jax.numpy as jnp
from jax import lax
from jax.experimental import pallas as pl
from jax.experimental.pallas import tpu as pltpu
from jax.sharding import Mesh
from jax.sharding import PartitionSpec as P

SENS = ("y", "x")
PTS = ("z", "core")
HIGH = lax.Precision.HIGHEST
REALS = 4
LANES = 128
BAND = 16
EXTRA = 16


def make_table(steps, freqs_count, padded):
    times = jnp.arange(steps, dtype=jnp.int32)
    freqs = jnp.arange(freqs_count, dtype=jnp.int32)
    phase = times[:, None] * freqs[None, :] % padded
    angle = phase.astype(jnp.float32) * (2.0 * math.pi / padded)
    edge = (freqs == 0) | (freqs == padded // 2)
    weights = jnp.where(edge, 1.0, 2.0).astype(jnp.float32) / padded
    both = jnp.concatenate([jnp.cos(angle) * weights, -jnp.sin(angle) * weights], axis=1)
    return jnp.pad(both, ((0, freqs_count - steps), (0, 0)))


def split(values):
    high = lax.reduce_precision(values, 8, 7)
    rest = values - high
    middle = lax.reduce_precision(rest, 8, 7)
    return jnp.stack([high, middle, rest - middle])


def scalar_rows(values, rows, columns):
    pieces = split(values).reshape(1, -1)
    return jnp.pad(pieces, ((0, rows - 1), (0, columns - pieces.shape[1]))).astype(jnp.bfloat16)


def read_scalars(block, count, reals):
    pieces = block[:, 0, : 3 * count * reals].astype(jnp.float32)
    return jnp.sum(pieces.reshape(-1, 3, count, reals), axis=(0, 1))


def to_all(block, axes, size):
    return lax.all_to_all(jnp.broadcast_to(block[None], (size,) + block.shape), axes, 0, 0)


def adjoint_kernel(series, table, tiles, extra, out, spec, *, unroll):
    sens, freqs = tiles.shape[1], tiles.shape[3]
    @pl.when(pl.program_id(0) == 0)
    def _():
        spec[...] = jnp.dot(series[...], table[...], preferred_element_type=jnp.float32, precision=HIGH)
        for k in range(out.shape[0]):
            out[k, pl.ds(out.shape[1] - EXTRA, EXTRA), :] = extra[...]
    band = pl.program_id(0)
    parts = out.shape[0] // (2 * REALS)
    bands = (out.shape[1] - EXTRA) // BAND
    for low in range(0, freqs, LANES):
        lanes = pl.ds(low, LANES)
        def step(i, acc):
            eight = pl.ds(pl.multiple_of(i * 8, 8), 8)
            real = spec[eight, lanes]
            imag = spec[eight, pl.ds(freqs + low, LANES)]
            acc = list(acc)
            for j in range(2):
                tr = tiles[0, 2 * i + j, :, lanes].astype(jnp.float32)
                ti = tiles[1, 2 * i + j, :, lanes].astype(jnp.float32)
                for b in range(REALS):
                    sr = real[4 * j + b : 4 * j + b + 1]
                    si = imag[4 * j + b : 4 * j + b + 1]
                    re, im = acc[b]
                    acc[b] = (re + (sr * tr + si * ti), im + (si * tr - sr * ti))
            return tuple(acc)
        zero = jnp.zeros((BAND, LANES), jnp.float32)
        acc = lax.fori_loop(0, sens // 2, step, ((zero, zero),) * REALS, unroll=unroll)
        for b in range(REALS):
            for c in range(2):
                low_row = pl.multiple_of(lax.rem(band, bands) * BAND, BAND)
                out[(c * REALS + b) * parts + band // bands, pl.ds(low_row, BAND), lanes] = acc[b][c].astype(jnp.bfloat16)

def adjoint(series, table, tiles, extra, senders, unroll=2):
    _, sens, points, freqs = tiles.shape
    shape = (senders, 2 * REALS * points // senders + EXTRA, freqs)
    return pl.pallas_call(
        functools.partial(adjoint_kernel, unroll=unroll),
        grid=(points // BAND,),
        in_specs=[
            pl.BlockSpec(series.shape, lambda i: (0, 0)),
            pl.BlockSpec(table.shape, lambda i: (0, 0)),
            pl.BlockSpec((2, sens, BAND, freqs), lambda i: (0, 0, i, 0)),
            pl.BlockSpec(extra.shape, lambda i: (0, 0)),
        ],
        out_specs=pl.BlockSpec(shape, lambda i: (0, 0, 0)),
        out_shape=jax.ShapeDtypeStruct(shape, jnp.bfloat16),
        scratch_shapes=[pltpu.VMEM((series.shape[0], 2 * freqs), jnp.float32)],
        name="adjoint",
    )(series, table, tiles, extra)

def fold(parts):
    place = lax.broadcasted_iota(jnp.int32, (8, LANES), 0)
    width = 4
    while len(parts) > 1:
        low = (place & width) == 0
        half = len(parts) // 2
        made = []
        for first, second in zip(parts[:half], parts[half:]):
            other = jnp.where(low, second, first)
            if width == 4:
                other = pltpu.roll(other, 4, 0)
            else:
                other = jnp.where(low, pltpu.roll(other, 8 - width, 0), pltpu.roll(other, width, 0))
            made.append(jnp.where(low, first, second) + other)
        parts = made
        width //= 2
    return parts[0]

def forward_kernel(weighted, table, tiles, out, wide, rows, *, per, unroll):
    points, freqs = tiles.shape[2], tiles.shape[3]
    step0 = pl.program_id(0)
    @pl.when(step0 == 0)
    def _():
        wide[...] = weighted[...].astype(jnp.float32)
    for low in range(0, freqs, LANES):
        lanes = pl.ds(low, LANES)
        def one(i, _):
            re = [None] * 8
            im = [None] * 8
            for p in range(0, points, 16):
                t2 = [[tiles[c, 2 * i + j, pl.ds(p, 16), lanes].astype(jnp.float32) for c in range(2)] for j in range(2)]
                for q in (0, 8):
                    for b in range(REALS):
                        wr = wide[0, b, pl.ds(p + q, 8), lanes]
                        wi = wide[1, b, pl.ds(p + q, 8), lanes]
                        for j in range(2):
                            tr = t2[j][0][q : q + 8]
                            ti = t2[j][1][q : q + 8]
                            k = 4 * j + b
                            x = wr * tr - wi * ti
                            y = wr * ti + wi * tr
                            re[k] = x if re[k] is None else re[k] + x
                            im[k] = y if im[k] is None else im[k] + y
            eight = pl.ds(pl.multiple_of((step0 * per + 2 * i) * 4, 8), 8)
            rows[eight, lanes] = fold(re)
            rows[eight, pl.ds(freqs + low, LANES)] = fold(im)
            return 0
        lax.fori_loop(0, per // 2, one, 0, unroll=unroll)
    @pl.when(step0 == pl.num_programs(0) - 1)
    def _():
        out[...] = lax.dot_general(rows[...], table[...], (((1,), (1,)), ((), ())), preferred_element_type=jnp.float32, precision=HIGH)

def forward(weighted, table, tiles, per=8, unroll=1):
    _, sens, points, freqs = tiles.shape
    return pl.pallas_call(
        functools.partial(forward_kernel, per=per, unroll=unroll),
        grid=(sens // per,),
        in_specs=[
            pl.BlockSpec(weighted.shape, lambda i: (0, 0, 0, 0)),
            pl.BlockSpec(table.shape, lambda i: (0, 0)),
            pl.BlockSpec((2, per, points, freqs), lambda i: (0, i, 0, 0)),
        ],
        out_specs=pl.BlockSpec((4 * sens, freqs), lambda i: (0, 0)),
        out_shape=jax.ShapeDtypeStruct((4 * sens, freqs), jnp.float32),
        scratch_shapes=[pltpu.VMEM(weighted.shape, jnp.float32), pltpu.VMEM((4 * sens, 2 * freqs), jnp.float32)],
        name="forward",
    )(weighted, table, tiles)


def on_device(records, tiles, gauges, prior, noise):
    reals, sensors, steps = records.shape
    points, freqs = prior.shape
    sites = gauges.shape[1]
    table = make_table(steps, freqs, 2 * steps)
    senders = lax.axis_size("y") * lax.axis_size("x")
    heights = lax.axis_size("z")
    place = lax.axis_index("y") * lax.axis_size("x") + lax.axis_index("x")
    core = lax.axis_index("core")
    chunk = 2 * reals * points // senders
    start = lax.rem(place * chunk, points)
    prior_chunk = lax.dynamic_slice(prior, (start, 0), (chunk, freqs))
    total_rows = reals * sensors
    rows = jnp.pad(records.transpose(1, 0, 2), ((0, 0), (0, 0), (0, freqs - steps)))
    rows = rows.reshape(total_rows, freqs)
    noisy = jnp.broadcast_to(noise[:, None], (sensors, reals)).reshape(total_rows, 1)

    def swap(block):
        return lax.ppermute(block, "core", [(0, 1), (1, 0)])

    def per_row(values):
        return jnp.broadcast_to(values[None], (sensors, reals)).reshape(total_rows, 1)

    def squares(first, second):
        sums = jnp.sum((first * second).reshape(-1, 8, freqs), axis=(0, 2))
        return jnp.sum(sums.reshape(-1, reals), axis=0)

    def point_sum(series, scalars):
        extra = scalar_rows(scalars, EXTRA, freqs)
        got = lax.all_to_all(adjoint(series, table, tiles, extra, senders), SENS, 0, 0)
        total = jnp.sum(got[:, :chunk].astype(jnp.float32), axis=0)
        return total, read_scalars(got[:, chunk:], scalars.shape[0], reals)

    def weigh(total):
        weighted = to_all((total * prior_chunk).astype(jnp.bfloat16), SENS, senders)
        weighted = weighted.reshape(2, reals, points, freqs)
        wide = weighted.astype(jnp.float32)
        return weighted, jnp.sum(wide * wide / prior[None, None], axis=(0, 2, 3))

    begin = jnp.stack([squares(rows, rows), squares(rows, rows * noisy)])
    points_0, (norm_0, noise_0) = point_sum(rows, begin)
    weighted_0, energy_0 = weigh(points_0)
    image = forward(weighted_0, table, tiles)
    half = total_rows // 2
    mine = lax.dynamic_slice(image, (core * half, 0), (half, freqs))
    other = lax.dynamic_slice(image, ((1 - core) * half, 0), (half, freqs))
    sent = jnp.concatenate([other, jnp.pad(energy_0[None], ((0, 7), (0, freqs - reals)))])
    got = swap(sent)
    pair = mine + got[:half]
    energy_pair = energy_0 + got[half, :reals]
    block = jnp.concatenate(
        [pair.astype(jnp.bfloat16), scalar_rows(energy_pair[None], EXTRA, freqs)]
    )
    got = to_all(block, "z", heights)
    mine = jnp.sum(got[:, :half].astype(jnp.float32), axis=0)
    energy_0 = read_scalars(got[:, half:], 1, reals)[0]
    theirs = swap(mine)
    image = jnp.where(core == 0, jnp.concatenate([mine, theirs]), jnp.concatenate([theirs, mine]))
    image = image + noisy * rows
    alpha_0 = norm_0 / (energy_0 + noise_0)
    residual = rows - per_row(alpha_0) * image

    begin = jnp.stack(
        [
            squares(residual, residual),
            squares(residual, residual * noisy),
            squares(residual, rows * noisy),
        ]
    )
    points_1, (norm_1, noise_1, noise_01) = point_sum(residual, begin)
    beta = norm_1 / norm_0
    mine_beta = lax.dynamic_index_in_dim(beta, lax.rem(place * chunk // points, reals), 0)
    points_1 = points_1 + mine_beta * points_0
    weighted_1, energy_1 = weigh(points_1)
    site_0 = forward(weighted_0, table, gauges, sites)
    site_1 = forward(weighted_1, table, gauges, sites)
    count = reals * sites
    block = jnp.concatenate(
        [site_0, site_1, jnp.pad(energy_1[None], ((0, 7), (0, freqs - reals)))]
    )
    block = block + swap(block)
    block = jnp.concatenate(
        [
            block[: 2 * count].astype(jnp.bfloat16),
            scalar_rows(block[2 * count : 2 * count + 1, :reals], EXTRA, freqs),
        ]
    )
    got = to_all(block, "z", heights)
    site_rows = jnp.sum(got[:, : 2 * count].astype(jnp.float32), axis=0)
    energy_1 = read_scalars(got[:, 2 * count :], 1, reals)[0]
    curve = energy_1 + noise_1 + 2.0 * beta * noise_01 + beta * beta * noise_0
    alpha_1 = norm_1 / curve
    direction = residual + per_row(beta) * rows
    estimate = per_row(alpha_0) * rows + per_row(alpha_1) * direction
    site_alpha_0 = jnp.broadcast_to(alpha_0[None], (sites, reals)).reshape(count, 1)
    site_alpha_1 = jnp.broadcast_to(alpha_1[None], (sites, reals)).reshape(count, 1)
    predicted = site_alpha_0 * site_rows[:count] + site_alpha_1 * site_rows[count:]

    def unrows(block, number):
        return block.reshape(number, reals, freqs).transpose(1, 0, 2)[:, :, :steps]

    return (unrows(estimate, sensors), unrows(predicted, sites))


def solution(mesh):
    fine = Mesh(mesh.devices.reshape(4, 4, 8, 2), SENS + PTS)
    return jax.shard_map(
        on_device,
        mesh=fine,
        in_specs=(
            P(None, SENS, None),
            P(None, SENS, PTS, None),
            P(None, SENS, PTS, None),
            P(PTS, None),
            P(SENS),
        ),
        out_specs=(P(None, SENS, None), P(None, SENS, None)),
        check_vma=False,
    )
```

```python
import functools

import jax
import jax.numpy as jnp
import numpy as np
from jax import lax
from jax.experimental import pallas as pl
from jax.experimental.pallas import tpu as pltpu
from jax.sharding import Mesh
from jax.sharding import PartitionSpec as P

SENS = ("y", "x")
PTS = ("z", "core")
REALS = 4
LANES = 128
BAND = 32
EXTRA = 16
F32 = jnp.float32
BF16 = jnp.bfloat16
VMEM = pl.BlockSpec(memory_space=pltpu.VMEM)
SMEM = pl.BlockSpec(memory_space=pltpu.SMEM)


def make_tables(freqs):
    padded = 2 * (freqs - 1)
    steps = np.arange(freqs, dtype=np.int64)
    angle = (steps[:, None] * steps[None, :] % padded) * (2.0 * np.pi / padded)
    both = np.concatenate([np.cos(angle), -np.sin(angle)], axis=1)
    high = both.astype(BF16)
    low = (both - high.astype(np.float64)).astype(BF16)
    weights = np.where((steps == 0) | (steps == freqs - 1), 1.0, 2.0) / padded
    weights = np.tile(weights[None], (8, 2)).astype(np.float32)
    return jnp.asarray(high), jnp.asarray(low), jnp.asarray(weights)


def product(left, high, low):
    first = left.astype(BF16)
    second = (left - first.astype(F32)).astype(BF16)

    def dot(a, b):
        return jnp.dot(a, b, preferred_element_type=F32)

    return dot(first, high) + (dot(first, low) + dot(second, high))


def lane_of(shape):
    return lax.broadcasted_iota(jnp.int32, shape, len(shape) - 1)


def three(values):
    first = values.astype(BF16).astype(F32)
    rest = values - first
    second = rest.astype(BF16).astype(F32)
    return first, second, rest - second


def write_scalars(out, columns):
    lane = lane_of((8, LANES))
    tile = jnp.zeros((8, LANES), F32)
    for k, column in enumerate(columns):
        tile = jnp.where(lane == k, column, tile)
    first, second, third = three(tile)
    tile = first + pltpu.roll(second, 32, 1) + pltpu.roll(third, 64, 1)
    block = jnp.concatenate([tile, jnp.zeros_like(tile)]).astype(BF16)
    rows = out.shape[1] - EXTRA
    for k in range(out.shape[0]):
        out[k, rows:, :] = block


def band_sum(first, second, start, count):
    total = jnp.zeros((8, first.shape[1]), F32)
    for row in range(start, start + count, 8):
        total = total + first[row : row + 8, :] * second[row : row + 8, :]
    return jnp.sum(total, axis=1, keepdims=True)


def send_points(series, tiles, high, low, weights, spec, out):
    sens, points, freqs = tiles.shape[1:]
    spec[...] = product(series[...], high[...], low[...]) * weights[0:1, :]
    blocks = freqs // LANES

    def part(index, _):
        band = index // blocks
        block = index % blocks
        lanes = pl.ds(pl.multiple_of(block * LANES, LANES), LANES)
        sines = pl.ds(pl.multiple_of(freqs + block * LANES, LANES), LANES)
        range_ = pl.ds(pl.multiple_of(band * BAND, BAND), BAND)

        def group(g, acc):
            acc = list(acc)
            rows = [pl.ds(pl.multiple_of(b * sens + g * 8, 8), 8) for b in range(REALS)]
            real = [spec[r, lanes] for r in rows]
            imag = [spec[r, sines] for r in rows]
            for j in range(8):
                tr = tiles[0, g * 8 + j, range_, lanes].astype(F32)
                ti = tiles[1, g * 8 + j, range_, lanes].astype(F32)
                for b in range(REALS):
                    sr = real[b][j : j + 1]
                    si = imag[b][j : j + 1]
                    re, im = acc[b]
                    acc[b] = (re + (sr * tr + si * ti), im + (si * tr - sr * ti))
            return tuple(acc)

        zero = jnp.zeros((BAND, LANES), F32)
        acc = lax.fori_loop(0, sens // 8, group, ((zero, zero),) * REALS)
        parts = points // BAND
        rows = pl.ds(pl.multiple_of(block * BAND, BAND), BAND)
        for b in range(REALS):
            for c in range(2):
                out[(c * REALS + b) * parts + band, rows, :] = acc[b][c].astype(BF16)
        return 0

    lax.fori_loop(0, (points // BAND) * blocks, part, 0)


def first_kernel(series, noise, tiles, high, low, weights, out, spec, *, sens):
    values = series[...]
    noisy = values * noise[...]
    columns = [band_sum(values, values, b * sens, sens) for b in range(REALS)]
    columns += [band_sum(values, noisy, b * sens, sens) for b in range(REALS)]
    write_scalars(out, columns)
    send_points(series, tiles, high, low, weights, spec, out)


def second_kernel(
    core, mine, theirs, series, noise, begin, tiles, high, low, weights, out, residual, alpha, image, spec
):
    half, freqs = mine.shape
    sens = 2 * half // REALS
    image[pl.ds(pl.multiple_of(core[0] * half, 8), half), :] = mine[...]
    image[pl.ds(pl.multiple_of((1 - core[0]) * half, 8), half), :] = theirs[...]
    lane = lane_of((8, LANES))
    tile = jnp.zeros((8, LANES), F32)
    real = lane_of((sens, freqs)) < freqs - 1
    last = freqs - 1
    columns = [[], [], []]
    for b in range(REALS):
        energy = image[b : b + 1, last:] + image[8 + b : 9 + b, last:] + image[16 + b : 17 + b, last:]
        scale = begin[0:1, b : b + 1] / (energy + begin[0:1, REALS + b : REALS + b + 1])
        tile = jnp.where(lane == b, scale, tile)
        rows = slice(b * sens, (b + 1) * sens)
        values = series[rows, :]
        noisy = noise[rows, :]
        left = values - scale * (jnp.where(real, image[rows, :], 0.0) + noisy * values)
        residual[rows, :] = left
        columns[0].append(band_sum(left, left, 0, sens))
        columns[1].append(band_sum(left, left * noisy, 0, sens))
        columns[2].append(band_sum(left, values * noisy, 0, sens))
    alpha[...] = tile
    write_scalars(out, columns[0] + columns[1] + columns[2])
    send_points(residual, tiles, high, low, weights, spec, out)


def sum_message(got):
    rows = got.shape[1] - EXTRA
    total = got[0, :rows, :].astype(F32)
    extra = got[0, rows:, :].astype(F32)
    for k in range(1, got.shape[0]):
        total = total + got[k, :rows, :].astype(F32)
        extra = extra + got[k, rows:, :].astype(F32)
    sums = jnp.broadcast_to(jnp.sum(extra, axis=0, keepdims=True), (8, LANES))
    sums = sums + pltpu.roll(sums, LANES - 32, 1) + pltpu.roll(sums, LANES - 64, 1)
    return total, sums


def put_weighted(total, prior, out):
    for block in range(prior.shape[1] // LANES):
        rows = slice(block * BAND, (block + 1) * BAND)
        lanes = slice(block * LANES, (block + 1) * LANES)
        part = (total[rows] * prior[:, lanes]).astype(BF16)
        for k in range(out.shape[0]):
            out[k, rows, :] = part


def weigh_kernel(got, prior, out, kept, sums_out):
    total, sums = sum_message(got)
    kept[...] = total
    sums_out[...] = sums
    put_weighted(total, prior, out)


def weigh_next_kernel(got, prior, before, begin, pick, out, sums_out):
    total, sums = sum_message(got)
    sums_out[...] = sums
    lane = lane_of((8, LANES))
    ratio = sums / jnp.where(lane < REALS, begin[...], 1.0)
    beta = jnp.sum(jnp.where(lane == pick[0], ratio, 0.0), axis=1, keepdims=True)[0:1]
    put_weighted(total + beta * before[...], prior, out)


def widen(weighted, prior, wide):
    energy = [jnp.zeros((8, LANES), F32)] * REALS
    parts = weighted.shape[0] // (2 * REALS)
    for h in range(parts):
        for block in range(prior.shape[1] // LANES):
            for row in range(0, BAND, 16):
                lanes = slice(block * LANES, (block + 1) * LANES)
                inverse = 1.0 / prior[h * BAND + row : h * BAND + row + 16, lanes]
                for b in range(REALS):
                    for c in range(2):
                        k = (c * REALS + b) * parts + h
                        at = slice(block * BAND + row, block * BAND + row + 16)
                        part = weighted[k, at, :].astype(F32)
                        wide[k, at, :] = part
                        term = part * part * inverse
                        energy[b] = energy[b] + (term[:8] + term[8:])
    return [
        jnp.sum(jnp.sum(e, axis=0, keepdims=True), axis=1, keepdims=True) for e in energy
    ]


def merge(first, second, width, place):
    low = (place & width) == 0
    other = jnp.where(low, second, first)
    if width == 4:
        other = pltpu.roll(other, 4, 0)
    else:
        other = jnp.where(low, pltpu.roll(other, 8 - width, 0), pltpu.roll(other, width, 0))
    return jnp.where(low, first, second) + other


def site_sums(tiles, wide, sites, reals, block, lanes):
    sums = {}
    for p in range(0, tiles.shape[2], 16):
        h, row = divmod(p, BAND)
        pair = [[tiles[c, s, pl.ds(p, 16), lanes].astype(F32) for c in range(2)] for s in sites]
        for q in (0, 8):
            for b in reals:
                at = pl.ds(pl.multiple_of(block * BAND + row + q, 8), 8)
                parts = tiles.shape[2] // BAND
                wr = wide[b * parts + h, at, :]
                wi = wide[(REALS + b) * parts + h, at, :]
                for j in range(len(sites)):
                    tr = pair[j][0][q : q + 8]
                    ti = pair[j][1][q : q + 8]
                    re = wr * tr - wi * ti
                    im = wr * ti + wi * tr
                    if (j, b) in sums:
                        re = sums[j, b][0] + re
                        im = sums[j, b][1] + im
                    sums[j, b] = (re, im)
    return sums


def synthesize(rows, weights, high, low, energy, stride):
    count, freqs = rows.shape[0], rows.shape[1] // 2
    scaled = rows[...] * weights[0:1, :]
    series = product(scaled[:, :freqs], high[:, :freqs], low[:, :freqs]) + product(
        scaled[:, freqs:], high[:, freqs:], low[:, freqs:]
    )
    row = lax.broadcasted_iota(jnp.int32, (count, freqs), 0)
    lane = lane_of((count, freqs))
    carried = jnp.zeros((count, 1), F32)
    index = row[:, 0:1]
    for b in range(REALS):
        hit = (index % stride == b) & (index < 3 * stride)
        carried = jnp.where(hit, energy[b], carried)
    return jnp.where(lane == freqs - 1, carried, series)


def forward_kernel(core, weighted, prior, tiles, high, low, weights, mine, other, wide, rows, full):
    sens, points, freqs = tiles.shape[1:]
    energy = widen(weighted, prior, wide)
    place = lax.broadcasted_iota(jnp.int32, (8, LANES), 0)
    blocks = freqs // LANES

    def part(index, _):
        g = index // blocks
        block = index % blocks
        lanes = pl.ds(pl.multiple_of(block * LANES, LANES), LANES)
        sines = pl.ds(pl.multiple_of(freqs + block * LANES, LANES), LANES)

        def pair(k):
            sums = site_sums(tiles, wide, [g * 8 + k, g * 8 + k + 4], range(REALS), block, lanes)
            return [
                [merge(sums[0, b][c], sums[1, b][c], 4, place) for c in range(2)]
                for b in range(REALS)
            ]

        def both(k):
            first = pair(k)
            second = pair(k + 2)
            return [
                [merge(first[b][c], second[b][c], 2, place) for c in range(2)]
                for b in range(REALS)
            ]

        first = both(0)
        second = both(1)
        for b in range(REALS):
            at = pl.ds(pl.multiple_of(b * sens + g * 8, 8), 8)
            rows[at, lanes] = merge(first[b][0], second[b][0], 1, place)
            rows[at, sines] = merge(first[b][1], second[b][1], 1, place)
        return 0

    lax.fori_loop(0, (sens // 8) * blocks, part, 0)
    half = REALS * sens // 2
    series = synthesize(rows, weights, high, low, energy + energy, 8)
    row = lax.broadcasted_iota(jnp.int32, (half, freqs), 0)
    lane = lane_of((half, freqs))
    carried = series[:half, freqs - 1 :]
    full[:half, :] = series[:half]
    full[half:, :] = jnp.where(lane == freqs - 1, carried, series[half:])
    mine[...] = full[pl.ds(pl.multiple_of(core[0] * half, 8), half), :]
    other[...] = full[pl.ds(pl.multiple_of((1 - core[0]) * half, 8), half), :]


def site_kernel(weighted, prior, tiles, high, low, weights, out, wide, rows):
    freqs = tiles.shape[3]
    energy = widen(weighted, prior, wide)
    place = lax.broadcasted_iota(jnp.int32, (8, LANES), 0)

    def part(block, _):
        lanes = pl.ds(pl.multiple_of(block * LANES, LANES), LANES)
        sines = pl.ds(pl.multiple_of(freqs + block * LANES, LANES), LANES)
        for low_b in range(0, REALS, 2):
            sums = site_sums(tiles, wide, range(4), (low_b, low_b + 1), block, lanes)
            for c, where in ((0, lanes), (1, sines)):
                blocks = [sums[j, low_b + b][c] for b in range(2) for j in range(4)]
                for width in (4, 2, 1):
                    half = len(blocks) // 2
                    blocks = [
                        merge(x, y, width, place) for x, y in zip(blocks[:half], blocks[half:])
                    ]
                rows[pl.ds(low_b * 4, 8), where] = blocks[0]
        return 0

    lax.fori_loop(0, freqs // LANES, part, 0)
    out[...] = synthesize(rows, weights, high, low, energy, REALS)


def spread_kernel(mine, got, out, *, stride, begin):
    values = mine[...] + got[...]
    count, freqs = values.shape
    row = lax.broadcasted_iota(jnp.int32, (count, freqs), 0) - begin
    carried = lane_of((count, freqs)) == freqs - 1
    _, second, third = three(values)
    second_row = (row >= stride) & (row < 2 * stride)
    third_row = (row >= 2 * stride) & (row < 3 * stride)
    values = jnp.where(carried & second_row, second, values)
    values = jnp.where(carried & third_row, third, values)
    block = values.astype(BF16)
    for k in range(out.shape[0]):
        out[k] = block


def sum_kernel(got, out):
    total = got[0].astype(F32)
    for k in range(1, got.shape[0]):
        total = total + got[k].astype(F32)
    out[...] = total


def last_kernel(got, begin, later, alpha, series, residual, estimate, predicted):
    reals, sens, steps = estimate.shape
    sites = predicted.shape[1]
    count = reals * sites
    total = got[0].astype(F32)
    for k in range(1, got.shape[0]):
        total = total + got[k].astype(F32)
    last = total.shape[1] - 1
    for b in range(reals):
        rows = [count + k * reals + b for k in range(3)]
        energy = sum(total[r : r + 1, last:] for r in rows)

        def value(ref, kind):
            return ref[0:1, kind * reals + b : kind * reals + b + 1]

        beta = value(later, 0) / value(begin, 0)
        curve = energy + value(later, 1) + 2.0 * beta * value(later, 2)
        curve = curve + beta * beta * value(begin, 1)
        first = value(alpha, 0)
        second = value(later, 0) / curve
        at = slice(b * sens, (b + 1) * sens)
        values = series[at, :]
        result = first * values + second * (residual[at, :] + beta * values)
        estimate[b] = result[:, :steps]
        low = total[b * sites : (b + 1) * sites]
        high = total[count + b * sites : count + (b + 1) * sites]
        predicted[b] = (first * low + second * high)[:, :steps]


def call(kernel, name, outs, scratch, specs, *args):
    return pl.pallas_call(
        kernel,
        in_specs=specs,
        out_specs=[VMEM] * len(outs),
        out_shape=[jax.ShapeDtypeStruct(*out) for out in outs],
        scratch_shapes=[pltpu.VMEM(*one) for one in scratch],
        compiler_params=pltpu.CompilerParams(vmem_limit_bytes=24 * 2**20),
        name=name,
    )(*args)


def on_device(records, tiles, gauges, prior, noise):
    reals, sensors, steps = records.shape
    points, freqs = prior.shape
    sites = gauges.shape[1]
    tables = make_tables(freqs)
    senders = lax.axis_size("y") * lax.axis_size("x")
    heights = lax.axis_size("z")
    place = lax.axis_index("y") * lax.axis_size("x") + lax.axis_index("x")
    core = lax.axis_index("core").astype(jnp.int32).reshape(1)
    start = lax.rem(place * BAND, points)
    prior_chunk = lax.dynamic_slice(prior, (start, 0), (BAND, freqs))
    pick = lax.rem(place * BAND // points, reals).astype(jnp.int32).reshape(1)
    count = reals * sensors
    half = count // 2
    series = jnp.pad(records, ((0, 0), (0, 0), (0, freqs - steps))).reshape(count, freqs)
    noisy = jnp.broadcast_to(noise[None, :], (reals, sensors)).reshape(count, 1)
    block_rows = BAND * freqs // LANES
    message = ((senders, block_rows + EXTRA, LANES), BF16)
    weighted_shape = (senders, block_rows, LANES)
    spectra = ((count, 2 * freqs), F32)
    rows = ((count, freqs), F32)
    tile = ((8, LANES), F32)

    def swap(block):
        return lax.ppermute(block, "core", [(0, 1), (1, 0)])

    (sent,) = call(
        functools.partial(first_kernel, sens=sensors),
        "first",
        [message],
        [spectra],
        [VMEM] * 6,
        *(series, noisy, tiles, *tables),
    )
    got = lax.all_to_all(sent, SENS, 0, 0)
    sent, points_0, begin = call(
        weigh_kernel,
        "weigh",
        [(weighted_shape, BF16), ((block_rows, LANES), F32), tile],
        [],
        [VMEM] * 2,
        *(got, prior_chunk),
    )
    weighted_0 = lax.all_to_all(sent, SENS, 0, 0)
    mine, other = call(
        forward_kernel,
        "forward",
        [((half, freqs), F32)] * 2,
        [(weighted_shape, F32), spectra, rows],
        [SMEM] + [VMEM] * 6,
        *(core, weighted_0, prior, tiles, *tables),
    )
    (sent,) = call(
        functools.partial(spread_kernel, stride=8, begin=0),
        "spread",
        [((heights, half, freqs), BF16)],
        [],
        [VMEM] * 2,
        *(mine, swap(other)),
    )
    got = lax.all_to_all(sent, "z", 0, 0)
    (mine,) = call(sum_kernel, "gather", [((half, freqs), F32)], [], [VMEM], got)
    theirs = swap(mine)
    sent, residual, alpha = call(
        second_kernel,
        "second",
        [message, rows, tile],
        [rows, spectra],
        [SMEM] + [VMEM] * 9,
        *(core, mine, theirs, series, noisy, begin, tiles, *tables),
    )
    got = lax.all_to_all(sent, SENS, 0, 0)
    sent, later = call(
        weigh_next_kernel,
        "weigh_next",
        [(weighted_shape, BF16), tile],
        [],
        [VMEM] * 4 + [SMEM],
        *(got, prior_chunk, points_0, begin, pick),
    )
    weighted_1 = lax.all_to_all(sent, SENS, 0, 0)

    def site(weighted, name):
        return call(
            site_kernel,
            name,
            [((reals * sites, freqs), F32)],
            [(weighted_shape, F32), ((reals * sites, 2 * freqs), F32)],
            [VMEM] * 6,
            *(weighted, prior, gauges, *tables),
        )[0]

    block = jnp.concatenate([site(weighted_0, "site_0"), site(weighted_1, "site_1")])
    (sent,) = call(
        functools.partial(spread_kernel, stride=reals, begin=reals * sites),
        "spread_sites",
        [((heights,) + block.shape, BF16)],
        [],
        [VMEM] * 2,
        *(block, swap(block)),
    )
    got = lax.all_to_all(sent, "z", 0, 0)
    estimate, predicted = call(
        last_kernel,
        "last",
        [((reals, sensors, steps), F32), ((reals, sites, steps), F32)],
        [],
        [VMEM] * 6,
        *(got, begin, later, alpha, series, residual),
    )
    return (estimate, predicted)


def solution(mesh):
    fine = Mesh(mesh.devices.reshape(4, 4, 8, 2), SENS + PTS)
    return jax.shard_map(
        on_device,
        mesh=fine,
        in_specs=(
            P(None, SENS, None),
            P(None, SENS, PTS, None),
            P(None, SENS, PTS, None),
            P(PTS, None),
            P(SENS),
        ),
        out_specs=(P(None, SENS, None), P(None, SENS, None)),
        check_vma=False,
    )
```

```python
import functools

import jax
import jax.numpy as jnp
import numpy as np
from jax import lax
from jax.experimental import pallas as pl
from jax.experimental.pallas import tpu as pltpu
from jax.sharding import Mesh
from jax.sharding import PartitionSpec as P

SENS = ("y", "x")
PTS = ("z", "core")
REALS = 4
LANES = 128
BAND = 32
EXTRA = 16
F32 = jnp.float32
BF16 = jnp.bfloat16
VMEM = pl.BlockSpec(memory_space=pltpu.VMEM)
HBM = pl.BlockSpec(memory_space=pltpu.HBM)
SMEM = pl.BlockSpec(memory_space=pltpu.SMEM)


def make_tables(freqs):
    padded = 2 * (freqs - 1)
    steps = np.arange(freqs, dtype=np.int64)
    angle = (steps[:, None] * steps[None, :] % padded) * (2.0 * np.pi / padded)
    both = np.concatenate([np.cos(angle), -np.sin(angle)], axis=1)
    high = both.astype(BF16)
    low = (both - high.astype(np.float64)).astype(BF16)
    return jnp.asarray(high), jnp.asarray(low)


def frequency_weights(freqs):
    at = lax.broadcasted_iota(jnp.int32, (1, 2 * freqs), 1)
    at = jnp.where(at < freqs, at, at - freqs)
    padded = 2 * (freqs - 1)
    return jnp.where((at == 0) | (at == freqs - 1), 1.0 / padded, 2.0 / padded)


def product(left, high, low):
    first = left.astype(BF16)
    second = (left - first.astype(F32)).astype(BF16)

    def dot(a, b):
        return jnp.dot(a, b, preferred_element_type=F32)

    return dot(first, high) + (dot(first, low) + dot(second, high))


def lane_of(shape):
    return lax.broadcasted_iota(jnp.int32, shape, len(shape) - 1)


def three(values):
    first = values.astype(BF16).astype(F32)
    rest = values - first
    second = rest.astype(BF16).astype(F32)
    return first, second, rest - second


def write_scalars(out, columns):
    lane = lane_of((8, LANES))
    tile = jnp.zeros((8, LANES), F32)
    for k, column in enumerate(columns):
        tile = jnp.where(lane == k, column, tile)
    first, second, third = three(tile)
    tile = first + pltpu.roll(second, 32, 1) + pltpu.roll(third, 64, 1)
    block = jnp.concatenate([tile, jnp.zeros_like(tile)]).astype(BF16)
    rows = out.shape[1] - EXTRA
    for k in range(out.shape[0]):
        out[k, rows:, :] = block


def band_sum(first, second, start, count):
    total = jnp.zeros((8, first.shape[1]), F32)
    for row in range(start, start + count, 8):
        total = total + first[row : row + 8, :] * second[row : row + 8, :]
    return jnp.sum(total, axis=1, keepdims=True)


def bands_of(source, target, done, first=0):
    def copy(band):
        at = pl.ds(pl.multiple_of(band * 16, 16), 16)
        return pltpu.make_async_copy(
            source.at[:, :, at, :], target.at[:, :, at, :], done.at[first + band]
        )

    return copy


def groups_of(source, target, done):
    def copy(group):
        at = pl.ds(group * 8, 8)
        return pltpu.make_async_copy(source.at[:, at], target.at[:, at], done.at[group])

    return copy


def send_points(series, tiles, copy, high, low, spec, out):
    sens, points, freqs = tiles.shape[1:]
    pair = product(series[...], high[...], low[...]) * frequency_weights(freqs)
    spec[:, : 2 * freqs] = pair
    spec[:, 2 * freqs :] = pair[:, :freqs] + pair[:, freqs:]
    blocks = freqs // LANES
    step = 16

    def part(index, _):
        band = index // blocks
        block = index % blocks
        lanes = [
            pl.ds(pl.multiple_of(c * freqs + block * LANES, LANES), LANES) for c in range(3)
        ]
        range_ = pl.ds(pl.multiple_of(band * step, step), step)

        @pl.when(block == 0)
        def _():
            copy(band).wait()

        def group(g, acc):
            acc = list(acc)
            rows = [pl.ds(pl.multiple_of(b * sens + g * 8, 8), 8) for b in range(REALS)]
            values = [[spec[r, c] for c in lanes] for r in rows]
            for j in range(8):
                tr = tiles[0, g * 8 + j, range_, lanes[0]].astype(F32)
                ti = tiles[1, g * 8 + j, range_, lanes[0]].astype(F32)
                terms = (tr, ti, tr - ti)
                for b in range(REALS):
                    acc[b] = tuple(
                        acc[b][c] + values[b][c][j : j + 1] * terms[c] for c in range(3)
                    )
            return tuple(acc)

        zero = jnp.zeros((step, LANES), F32)
        acc = lax.fori_loop(0, sens // 8, group, ((zero, zero, zero),) * REALS)
        per = BAND // step
        parts = points // BAND
        at = pl.ds(pl.multiple_of(block * BAND + (band % per) * step, step), step)
        for b in range(REALS):
            first, second, third = acc[b]
            out[b * parts + band // per, at, :] = (first + second).astype(BF16)
            out[(REALS + b) * parts + band // per, at, :] = (third - first + second).astype(BF16)
        return 0

    lax.fori_loop(0, (points // step) * blocks, part, 0)


def first_kernel(
    records, noise, tiles_in, high_in, low_in, out, series, column, raw, raw_noise, tiles, high, low, spec, done
):
    reals, sens, steps = records.shape
    moves = ((records, raw), (noise, raw_noise), (high_in, high), (low_in, low))
    copies = [pltpu.make_async_copy(*move, done.at[k]) for k, move in enumerate(moves)]
    fetch = bands_of(tiles_in, tiles, done, len(copies))
    for copy in copies + [fetch(k) for k in range(tiles.shape[2] // 16)]:
        copy.start()
    copies[0].wait()
    copies[1].wait()
    row = lax.broadcasted_iota(jnp.int32, (sens, sens), 0)
    noises = jnp.where(row == lane_of((sens, sens)), raw_noise[...], 0.0)
    noises = jnp.sum(noises, axis=1, keepdims=True)
    column[...] = noises
    series[...] = jnp.zeros_like(series)
    columns = [[], []]
    for b in range(reals):
        series[b * sens : (b + 1) * sens, :steps] = raw[b]
    for b in range(reals):
        values = series[b * sens : (b + 1) * sens, :]
        columns[0].append(band_sum(values, values, 0, sens))
        columns[1].append(band_sum(values, values * noises, 0, sens))
    write_scalars(out, columns[0] + columns[1])
    copies[2].wait()
    copies[3].wait()
    send_points(series, tiles, fetch, high, low, spec, out)


def second_kernel(
    core, mine, theirs, series, noise, begin, tiles_in, high, low, out, residual, alpha, image, tiles, spec, done
):
    fetch = bands_of(tiles_in, tiles, done)
    for k in range(tiles.shape[2] // 16):
        fetch(k).start()
    half, freqs = mine.shape
    sens = 2 * half // REALS
    image[pl.ds(pl.multiple_of(core[0] * half, 8), half), :] = mine[...]
    image[pl.ds(pl.multiple_of((1 - core[0]) * half, 8), half), :] = theirs[...]
    lane = lane_of((8, LANES))
    tile = jnp.zeros((8, LANES), F32)
    real = lane_of((sens, freqs)) < freqs - 1
    last = freqs - 1
    columns = [[], [], []]
    for b in range(REALS):
        energy = image[b : b + 1, last:] + image[8 + b : 9 + b, last:] + image[16 + b : 17 + b, last:]
        scale = begin[0:1, b : b + 1] / (energy + begin[0:1, REALS + b : REALS + b + 1])
        tile = jnp.where(lane == b, scale, tile)
        rows = slice(b * sens, (b + 1) * sens)
        values = series[rows, :]
        noisy = noise[...]
        left = values - scale * (jnp.where(real, image[rows, :], 0.0) + noisy * values)
        residual[rows, :] = left
        columns[0].append(band_sum(left, left, 0, sens))
        columns[1].append(band_sum(left, left * noisy, 0, sens))
        columns[2].append(band_sum(left, values * noisy, 0, sens))
    alpha[...] = tile
    write_scalars(out, columns[0] + columns[1] + columns[2])
    send_points(residual, tiles, fetch, high, low, spec, out)


def sum_message(got):
    rows = got.shape[1] - EXTRA
    total = got[0, :rows, :].astype(F32)
    extra = got[0, rows:, :].astype(F32)
    for k in range(1, got.shape[0]):
        total = total + got[k, :rows, :].astype(F32)
        extra = extra + got[k, rows:, :].astype(F32)
    sums = jnp.broadcast_to(jnp.sum(extra, axis=0, keepdims=True), (8, LANES))
    sums = sums + pltpu.roll(sums, LANES - 32, 1) + pltpu.roll(sums, LANES - 64, 1)
    return total, sums


def put_weighted(total, prior, out):
    for block in range(prior.shape[1] // LANES):
        rows = slice(block * BAND, (block + 1) * BAND)
        lanes = slice(block * LANES, (block + 1) * LANES)
        part = (total[rows] * prior[:, lanes]).astype(BF16)
        for k in range(out.shape[0]):
            out[k, rows, :] = part


def weigh_kernel(got, prior, out, kept, sums_out):
    total, sums = sum_message(got)
    kept[...] = total
    sums_out[...] = sums
    put_weighted(total, prior, out)


def weigh_next_kernel(got, prior, before, begin, pick, out, sums_out):
    total, sums = sum_message(got)
    sums_out[...] = sums
    lane = lane_of((8, LANES))
    ratio = sums / jnp.where(lane < REALS, begin[...], 1.0)
    beta = jnp.sum(jnp.where(lane == pick[0], ratio, 0.0), axis=1, keepdims=True)[0:1]
    put_weighted(total + beta * before[...], prior, out)


def widen(weighted, prior, wide):
    energy = [jnp.zeros((8, LANES), F32)] * REALS
    parts = weighted.shape[0] // (2 * REALS)
    for h in range(parts):
        for block in range(prior.shape[1] // LANES):
            for row in range(0, BAND, 16):
                lanes = slice(block * LANES, (block + 1) * LANES)
                inverse = 1.0 / prior[h * BAND + row : h * BAND + row + 16, lanes]
                for b in range(REALS):
                    at = slice(block * BAND + row, block * BAND + row + 16)
                    re = weighted[b * parts + h, at, :].astype(F32)
                    im = weighted[(REALS + b) * parts + h, at, :].astype(F32)
                    wide[b * parts + h, at, :] = re
                    wide[(REALS + b) * parts + h, at, :] = im
                    wide[(2 * REALS + b) * parts + h, at, :] = re + im
                    term = (re * re + im * im) * inverse
                    energy[b] = energy[b] + (term[:8] + term[8:])
    return [
        jnp.sum(jnp.sum(e, axis=0, keepdims=True), axis=1, keepdims=True) for e in energy
    ]


def merge(first, second, width, place):
    low = (place & width) == 0
    other = jnp.where(low, second, first)
    if width == 4:
        other = pltpu.roll(other, 4, 0)
    else:
        other = jnp.where(low, pltpu.roll(other, 8 - width, 0), pltpu.roll(other, width, 0))
    return jnp.where(low, first, second) + other


def site_sums(tiles, wide, sites, reals, block, lanes):
    sums = {}
    parts = tiles.shape[2] // BAND
    for p in range(0, tiles.shape[2], 16):
        h, row = divmod(p, BAND)
        terms = []
        for s in sites:
            tr, ti = (tiles[c, s, pl.ds(p, 16), lanes].astype(F32) for c in range(2))
            terms.append((tr, ti, tr + ti))
        for q in (0, 8):
            at = pl.ds(pl.multiple_of(block * BAND + row + q, 8), 8)
            for b in reals:
                values = [wide[(c * REALS + b) * parts + h, at, :] for c in range(3)]
                for j in range(len(sites)):
                    new = [values[c] * terms[j][c][q : q + 8] for c in range(3)]
                    if (j, b) in sums:
                        new = [x + y for x, y in zip(sums[j, b], new)]
                    sums[j, b] = new
    return {k: (x - y, z - x - y) for k, (x, y, z) in sums.items()}


def synthesize(rows, high, low, energy, stride):
    count, freqs = rows.shape[0], rows.shape[1] // 2
    scaled = rows[...] * frequency_weights(freqs)
    series = product(scaled[:, :freqs], high[:, :freqs], low[:, :freqs]) + product(
        scaled[:, freqs:], high[:, freqs:], low[:, freqs:]
    )
    row = lax.broadcasted_iota(jnp.int32, (count, freqs), 0)
    lane = lane_of((count, freqs))
    carried = jnp.zeros((count, 1), F32)
    index = row[:, 0:1]
    for b in range(REALS):
        hit = (index % stride == b) & (index < 3 * stride)
        carried = jnp.where(hit, energy[b], carried)
    return jnp.where(lane == freqs - 1, carried, series)


def forward_kernel(
    core, weighted, prior, tiles_in, high, low, mine, other, wide, rows, full, tiles, done
):
    sens, points, freqs = tiles.shape[1:]
    fetch = groups_of(tiles_in, tiles, done)
    for k in range(sens // 8):
        fetch(k).start()
    energy = widen(weighted, prior, wide)
    place = lax.broadcasted_iota(jnp.int32, (8, LANES), 0)
    blocks = freqs // LANES

    def part(index, _):
        g = index // blocks
        block = index % blocks
        lanes = pl.ds(pl.multiple_of(block * LANES, LANES), LANES)
        sines = pl.ds(pl.multiple_of(freqs + block * LANES, LANES), LANES)

        @pl.when(block == 0)
        def _():
            fetch(g).wait()

        def pair(k):
            sums = site_sums(tiles, wide, [g * 8 + k, g * 8 + k + 4], range(REALS), block, lanes)
            return [
                [merge(sums[0, b][c], sums[1, b][c], 4, place) for c in range(2)]
                for b in range(REALS)
            ]

        def both(k):
            first = pair(k)
            second = pair(k + 2)
            return [
                [merge(first[b][c], second[b][c], 2, place) for c in range(2)]
                for b in range(REALS)
            ]

        first = both(0)
        second = both(1)
        for b in range(REALS):
            at = pl.ds(pl.multiple_of(b * sens + g * 8, 8), 8)
            rows[at, lanes] = merge(first[b][0], second[b][0], 1, place)
            rows[at, sines] = merge(first[b][1], second[b][1], 1, place)
        return 0

    lax.fori_loop(0, (sens // 8) * blocks, part, 0)
    half = REALS * sens // 2
    series = synthesize(rows, high, low, energy + energy, 8)
    row = lax.broadcasted_iota(jnp.int32, (half, freqs), 0)
    lane = lane_of((half, freqs))
    carried = series[:half, freqs - 1 :]
    full[:half, :] = series[:half]
    full[half:, :] = jnp.where(lane == freqs - 1, carried, series[half:])
    mine[...] = full[pl.ds(pl.multiple_of(core[0] * half, 8), half), :]
    other[...] = full[pl.ds(pl.multiple_of((1 - core[0]) * half, 8), half), :]


def site_kernel(weighted, prior, tiles, high, low, out, wide, rows):
    freqs = tiles.shape[3]
    energy = widen(weighted, prior, wide)
    place = lax.broadcasted_iota(jnp.int32, (8, LANES), 0)

    def part(block, _):
        lanes = pl.ds(pl.multiple_of(block * LANES, LANES), LANES)
        sines = pl.ds(pl.multiple_of(freqs + block * LANES, LANES), LANES)
        for low_b in range(0, REALS, 2):
            sums = site_sums(tiles, wide, range(4), (low_b, low_b + 1), block, lanes)
            for c, where in ((0, lanes), (1, sines)):
                blocks = [sums[j, low_b + b][c] for b in range(2) for j in range(4)]
                for width in (4, 2, 1):
                    half = len(blocks) // 2
                    blocks = [
                        merge(x, y, width, place) for x, y in zip(blocks[:half], blocks[half:])
                    ]
                rows[pl.ds(low_b * 4, 8), where] = blocks[0]
        return 0

    lax.fori_loop(0, freqs // LANES, part, 0)
    out[...] = synthesize(rows, high, low, energy, REALS)


def spread_kernel(mine, got, out, *, stride, begin):
    values = mine[...] + got[...]
    count, freqs = values.shape
    row = lax.broadcasted_iota(jnp.int32, (count, freqs), 0) - begin
    carried = lane_of((count, freqs)) == freqs - 1
    _, second, third = three(values)
    second_row = (row >= stride) & (row < 2 * stride)
    third_row = (row >= 2 * stride) & (row < 3 * stride)
    values = jnp.where(carried & second_row, second, values)
    values = jnp.where(carried & third_row, third, values)
    block = values.astype(BF16)
    for k in range(out.shape[0]):
        out[k] = block


def sum_kernel(got, out):
    total = got[0].astype(F32)
    for k in range(1, got.shape[0]):
        total = total + got[k].astype(F32)
    out[...] = total


def last_kernel(got, begin, later, alpha, series, residual, estimate, predicted):
    reals, sens, steps = estimate.shape
    sites = predicted.shape[1]
    count = reals * sites
    total = got[0].astype(F32)
    for k in range(1, got.shape[0]):
        total = total + got[k].astype(F32)
    last = total.shape[1] - 1
    for b in range(reals):
        rows = [count + k * reals + b for k in range(3)]
        energy = sum(total[r : r + 1, last:] for r in rows)

        def value(ref, kind):
            return ref[0:1, kind * reals + b : kind * reals + b + 1]

        beta = value(later, 0) / value(begin, 0)
        curve = energy + value(later, 1) + 2.0 * beta * value(later, 2)
        curve = curve + beta * beta * value(begin, 1)
        first = value(alpha, 0)
        second = value(later, 0) / curve
        at = slice(b * sens, (b + 1) * sens)
        values = series[at, :]
        result = first * values + second * (residual[at, :] + beta * values)
        estimate[b] = result[:, :steps]
        low = total[b * sites : (b + 1) * sites]
        high = total[count + b * sites : count + (b + 1) * sites]
        predicted[b] = (first * low + second * high)[:, :steps]


def in_hbm(array):
    return pltpu.with_memory_space_constraint(array, pltpu.HBM)


def call(kernel, name, outs, scratch, specs, *args, semaphores=0, limit=24 * 2**20):
    scratch = [pltpu.VMEM(*one) for one in scratch]
    args = [in_hbm(arg) if spec is HBM else arg for arg, spec in zip(args, specs)]
    if semaphores:
        scratch.append(pltpu.SemaphoreType.DMA((semaphores,)))
    return pl.pallas_call(
        kernel,
        in_specs=specs,
        out_specs=[VMEM] * len(outs),
        out_shape=[jax.ShapeDtypeStruct(*out) for out in outs],
        scratch_shapes=scratch,
        compiler_params=pltpu.CompilerParams(vmem_limit_bytes=limit),
        name=name,
    )(*args)


def on_device(records, tiles, gauges, prior, noise):
    reals, sensors, steps = records.shape
    points, freqs = prior.shape
    sites = gauges.shape[1]
    tables = make_tables(freqs)
    senders = lax.axis_size("y") * lax.axis_size("x")
    heights = lax.axis_size("z")
    place = lax.axis_index("y") * lax.axis_size("x") + lax.axis_index("x")
    core = lax.axis_index("core").astype(jnp.int32).reshape(1)
    start = lax.rem(place * BAND, points)
    prior_chunk = lax.dynamic_slice(prior, (start, 0), (BAND, freqs))
    pick = lax.rem(place * BAND // points, reals).astype(jnp.int32).reshape(1)
    count = reals * sensors
    half = count // 2
    block_rows = BAND * freqs // LANES
    message = ((senders, block_rows + EXTRA, LANES), BF16)
    weighted_shape = (senders, block_rows, LANES)
    wide_shape = (3 * senders // 2, block_rows, LANES)
    spectra = ((count, 2 * freqs), F32)
    sums = ((count, 3 * freqs), F32)
    rows = ((count, freqs), F32)
    tile = ((8, LANES), F32)

    def swap(block):
        return lax.ppermute(block, "core", [(0, 1), (1, 0)])

    bands = points // 16
    local = (tiles.shape, BF16)
    sent, series, noisy = call(
        first_kernel,
        "first",
        [message, rows, ((sensors, 1), F32)],
        [(records.shape, F32), ((1, sensors), F32), local]
        + [(table.shape, BF16) for table in tables]
        + [sums],
        [HBM] * 5,
        *(records, noise.reshape(1, sensors), tiles, *tables),
        semaphores=4 + bands,
    )
    got = lax.all_to_all(sent, SENS, 0, 0)
    sent, points_0, begin = call(
        weigh_kernel,
        "weigh",
        [(weighted_shape, BF16), ((block_rows, LANES), F32), tile],
        [],
        [VMEM] * 2,
        *(got, prior_chunk),
    )
    weighted_0 = lax.all_to_all(sent, SENS, 0, 0)
    mine, other = call(
        forward_kernel,
        "forward",
        [((half, freqs), F32)] * 2,
        [(wide_shape, F32), spectra, rows, local],
        [SMEM, VMEM, VMEM, HBM, VMEM, VMEM],
        *(core, weighted_0, prior, tiles, *tables),
        semaphores=sensors // 8,
    )
    (sent,) = call(
        functools.partial(spread_kernel, stride=8, begin=0),
        "spread",
        [((heights, half, freqs), BF16)],
        [],
        [VMEM] * 2,
        *(mine, swap(other)),
    )
    got = lax.all_to_all(sent, "z", 0, 0)
    (mine,) = call(sum_kernel, "gather", [((half, freqs), F32)], [], [VMEM], got)
    theirs = swap(mine)
    sent, residual, alpha = call(
        second_kernel,
        "second",
        [message, rows, tile],
        [rows, local, sums],
        [SMEM] + [VMEM] * 5 + [HBM, VMEM, VMEM],
        *(core, mine, theirs, series, noisy, begin, tiles, *tables),
        semaphores=bands,
    )
    got = lax.all_to_all(sent, SENS, 0, 0)
    sent, later = call(
        weigh_next_kernel,
        "weigh_next",
        [(weighted_shape, BF16), tile],
        [],
        [VMEM] * 4 + [SMEM],
        *(got, prior_chunk, points_0, begin, pick),
    )
    weighted_1 = lax.all_to_all(sent, SENS, 0, 0)

    def site(weighted, name):
        return call(
            site_kernel,
            name,
            [((reals * sites, freqs), F32)],
            [(wide_shape, F32), ((reals * sites, 2 * freqs), F32)],
            [VMEM] * 5,
            *(weighted, prior, gauges, *tables),
        )[0]

    block = jnp.concatenate([site(weighted_0, "site_0"), site(weighted_1, "site_1")])
    (sent,) = call(
        functools.partial(spread_kernel, stride=reals, begin=reals * sites),
        "spread_sites",
        [((heights,) + block.shape, BF16)],
        [],
        [VMEM] * 2,
        *(block, swap(block)),
    )
    got = lax.all_to_all(sent, "z", 0, 0)
    estimate, predicted = call(
        last_kernel,
        "last",
        [((reals, sensors, steps), F32), ((reals, sites, steps), F32)],
        [],
        [VMEM] * 6,
        *(got, begin, later, alpha, series, residual),
    )
    return (estimate, predicted)


def solution(mesh):
    fine = Mesh(mesh.devices.reshape(4, 4, 8, 2), SENS + PTS)
    return jax.shard_map(
        on_device,
        mesh=fine,
        in_specs=(
            P(None, SENS, None),
            P(None, SENS, PTS, None),
            P(None, SENS, PTS, None),
            P(PTS, None),
            P(SENS),
        ),
        out_specs=(P(None, SENS, None), P(None, SENS, None)),
        check_vma=False,
    )
```

```python
import functools

import jax
import jax.numpy as jnp
import numpy as np
from jax import lax
from jax.experimental import pallas as pl
from jax.experimental.pallas import tpu as pltpu
from jax.sharding import Mesh
from jax.sharding import PartitionSpec as P

SENS = ("y", "x")
PTS = ("z", "core")
REALS = 4
LANES = 128
BAND = 32
EXTRA = 16
F32 = jnp.float32
BF16 = jnp.bfloat16
VMEM = pl.BlockSpec(memory_space=pltpu.VMEM)
HBM = pl.BlockSpec(memory_space=pltpu.HBM)
SMEM = pl.BlockSpec(memory_space=pltpu.SMEM)


def make_tables(freqs):
    padded = 2 * (freqs - 1)
    steps = np.arange(freqs, dtype=np.int64)
    angle = (steps[:, None] * steps[None, :] % padded) * (2.0 * np.pi / padded)
    both = np.concatenate([np.cos(angle), -np.sin(angle)], axis=1)
    high = both.astype(BF16)
    low = (both - high.astype(np.float64)).astype(BF16)
    return jnp.asarray(high), jnp.asarray(low)


def frequency_weights(freqs):
    at = lax.broadcasted_iota(jnp.int32, (1, 2 * freqs), 1)
    at = jnp.where(at < freqs, at, at - freqs)
    padded = 2 * (freqs - 1)
    return jnp.where((at == 0) | (at == freqs - 1), 1.0 / padded, 2.0 / padded)


def product(left, high, low):
    first = left.astype(BF16)
    second = (left - first.astype(F32)).astype(BF16)

    def dot(a, b):
        return jnp.dot(a, b, preferred_element_type=F32)

    return dot(first, high) + (dot(first, low) + dot(second, high))


def lane_of(shape):
    return lax.broadcasted_iota(jnp.int32, shape, len(shape) - 1)


def three(values):
    first = values.astype(BF16).astype(F32)
    rest = values - first
    second = rest.astype(BF16).astype(F32)
    return first, second, rest - second


def write_scalars(out, columns):
    lane = lane_of((8, LANES))
    tile = jnp.zeros((8, LANES), F32)
    for k, column in enumerate(columns):
        tile = jnp.where(lane == k, column, tile)
    first, second, third = three(tile)
    tile = first + pltpu.roll(second, 32, 1) + pltpu.roll(third, 64, 1)
    block = jnp.concatenate([tile, jnp.zeros_like(tile)]).astype(BF16)
    rows = out.shape[1] - EXTRA
    for k in range(out.shape[0]):
        out[k, rows:, :] = block


def band_sum(first, second, start, count):
    total = jnp.zeros((8, first.shape[1]), F32)
    for row in range(start, start + count, 8):
        total = total + first[row : row + 8, :] * second[row : row + 8, :]
    return jnp.sum(total, axis=1, keepdims=True)


def pieces_of(source, target, done, first=0):
    groups = source.shape[1] // 8

    def copy(band, group):
        at = (slice(None), pl.ds(group * 8, 8), pl.ds(pl.multiple_of(band * BAND, BAND), BAND))
        return pltpu.make_async_copy(
            source.at[at], target.at[at], done.at[first + band * groups + group]
        )

    copies = [copy(b, g) for b in range(source.shape[2] // BAND) for g in range(groups)]
    return copy, copies


def groups_of(source, target, done):
    def copy(group):
        at = pl.ds(group * 8, 8)
        return pltpu.make_async_copy(source.at[:, at], target.at[:, at], done.at[group])

    return copy


def send_points(series, tiles, copy, high, low, spec, stage, out, gone):
    sens, points, freqs = tiles.shape[1:]
    spec[...] = product(series[...], high[...], low[...]) * frequency_weights(freqs)
    blocks = freqs // LANES

    def part(index, _):
        band = index // blocks
        block = index % blocks
        lanes = pl.ds(pl.multiple_of(block * LANES, LANES), LANES)
        sines = pl.ds(pl.multiple_of(freqs + block * LANES, LANES), LANES)
        range_ = pl.ds(pl.multiple_of(band * BAND, BAND), BAND)

        def group(g, acc):
            @pl.when(block == 0)
            def _():
                copy(band, g).wait()

            acc = list(acc)
            rows = [pl.ds(pl.multiple_of(b * sens + g * 8, 8), 8) for b in range(REALS)]
            real = [spec[r, lanes] for r in rows]
            imag = [spec[r, sines] for r in rows]
            for j in range(8):
                tr = tiles[0, g * 8 + j, range_, lanes].astype(F32)
                ti = tiles[1, g * 8 + j, range_, lanes].astype(F32)
                for b in range(REALS):
                    sr = real[b][j : j + 1]
                    si = imag[b][j : j + 1]
                    re, im = acc[b]
                    acc[b] = (re + (sr * tr + si * ti), im + (si * tr - sr * ti))
            return tuple(acc)

        zero = jnp.zeros((BAND, LANES), F32)
        acc = lax.fori_loop(0, sens // 8, group, ((zero, zero),) * REALS)
        rows = pl.ds(pl.multiple_of(block * BAND, BAND), BAND)
        for b in range(REALS):
            for c in range(2):
                stage[band * 2 * REALS + c * REALS + b, rows, :] = acc[b][c].astype(BF16)
        send(index).start()
        return 0

    def send(index):
        band = index // blocks
        rows = pl.ds(pl.multiple_of((index % blocks) * BAND, BAND), BAND)
        at = (pl.ds(band * 2 * REALS, 2 * REALS), rows)
        return pltpu.make_async_copy(stage.at[at], out.at[at], gone.at[index])

    number = (points // BAND) * blocks
    at = (slice(None), pl.ds(blocks * BAND, EXTRA))
    scalars = pltpu.make_async_copy(stage.at[at], out.at[at], gone.at[number])
    scalars.start()
    lax.fori_loop(0, number, part, 0)
    for index in range(number):
        send(index).wait()
    scalars.wait()


def first_kernel(
    records, noise, tiles_in, high_in, low_in, out, series, column, high, low, raw, raw_noise, tiles, spec, stage, done, gone
):
    reals, sens, steps = records.shape
    moves = ((records, raw), (noise, raw_noise), (high_in, high), (low_in, low))
    copies = [pltpu.make_async_copy(*move, done.at[k]) for k, move in enumerate(moves)]
    fetch, pieces = pieces_of(tiles_in, tiles, done, len(copies))
    for copy in copies + pieces:
        copy.start()
    copies[0].wait()
    copies[1].wait()
    row = lax.broadcasted_iota(jnp.int32, (sens, sens), 0)
    noises = jnp.where(row == lane_of((sens, sens)), raw_noise[...], 0.0)
    noises = jnp.sum(noises, axis=1, keepdims=True)
    column[...] = noises
    series[...] = jnp.zeros_like(series)
    columns = [[], []]
    for b in range(reals):
        series[b * sens : (b + 1) * sens, :steps] = raw[b]
    for b in range(reals):
        values = series[b * sens : (b + 1) * sens, :]
        columns[0].append(band_sum(values, values, 0, sens))
        columns[1].append(band_sum(values, values * noises, 0, sens))
    write_scalars(stage, columns[0] + columns[1])
    copies[2].wait()
    copies[3].wait()
    send_points(series, tiles, fetch, high, low, spec, stage, out, gone)


def second_kernel(
    core, mine, theirs, series, noise, begin, tiles_in, high, low, out, residual, alpha, image, tiles, spec, stage, done, gone
):
    fetch, pieces = pieces_of(tiles_in, tiles, done)
    for copy in pieces:
        copy.start()
    half, freqs = mine.shape
    sens = 2 * half // REALS
    image[pl.ds(pl.multiple_of(core[0] * half, 8), half), :] = mine[...]
    image[pl.ds(pl.multiple_of((1 - core[0]) * half, 8), half), :] = theirs[...]
    lane = lane_of((8, LANES))
    tile = jnp.zeros((8, LANES), F32)
    real = lane_of((sens, freqs)) < freqs - 1
    last = freqs - 1
    columns = [[], [], []]
    for b in range(REALS):
        energy = image[b : b + 1, last:] + image[8 + b : 9 + b, last:] + image[16 + b : 17 + b, last:]
        scale = begin[0:1, b : b + 1] / (energy + begin[0:1, REALS + b : REALS + b + 1])
        tile = jnp.where(lane == b, scale, tile)
        rows = slice(b * sens, (b + 1) * sens)
        values = series[rows, :]
        noisy = noise[...]
        left = values - scale * (jnp.where(real, image[rows, :], 0.0) + noisy * values)
        residual[rows, :] = left
        columns[0].append(band_sum(left, left, 0, sens))
        columns[1].append(band_sum(left, left * noisy, 0, sens))
        columns[2].append(band_sum(left, values * noisy, 0, sens))
    alpha[...] = tile
    write_scalars(stage, columns[0] + columns[1] + columns[2])
    send_points(residual, tiles, fetch, high, low, spec, stage, out, gone)


def sum_message(got):
    rows = got.shape[1] - EXTRA
    total = got[0, :rows, :].astype(F32)
    extra = got[0, rows:, :].astype(F32)
    for k in range(1, got.shape[0]):
        total = total + got[k, :rows, :].astype(F32)
        extra = extra + got[k, rows:, :].astype(F32)
    sums = jnp.broadcast_to(jnp.sum(extra, axis=0, keepdims=True), (8, LANES))
    sums = sums + pltpu.roll(sums, LANES - 32, 1) + pltpu.roll(sums, LANES - 64, 1)
    return total, sums


def put_weighted(total, prior, out):
    for block in range(prior.shape[1] // LANES):
        rows = slice(block * BAND, (block + 1) * BAND)
        lanes = slice(block * LANES, (block + 1) * LANES)
        part = (total[rows] * prior[:, lanes]).astype(BF16)
        for k in range(out.shape[0]):
            out[k, rows, :] = part


def weigh_kernel(got, prior, out, kept, sums_out):
    total, sums = sum_message(got)
    kept[...] = total
    sums_out[...] = sums
    put_weighted(total, prior, out)


def weigh_next_kernel(got, prior, before, begin, pick, out, sums_out):
    total, sums = sum_message(got)
    sums_out[...] = sums
    lane = lane_of((8, LANES))
    ratio = sums / jnp.where(lane < REALS, begin[...], 1.0)
    beta = jnp.sum(jnp.where(lane == pick[0], ratio, 0.0), axis=1, keepdims=True)[0:1]
    put_weighted(total + beta * before[...], prior, out)


def widen(weighted, prior, wide):
    energy = [jnp.zeros((8, LANES), F32)] * REALS
    parts = weighted.shape[0] // (2 * REALS)
    for h in range(parts):
        for block in range(prior.shape[1] // LANES):
            for row in range(0, BAND, 16):
                lanes = slice(block * LANES, (block + 1) * LANES)
                inverse = 1.0 / prior[h * BAND + row : h * BAND + row + 16, lanes]
                for b in range(REALS):
                    at = slice(block * BAND + row, block * BAND + row + 16)
                    re = weighted[h * 2 * REALS + b, at, :].astype(F32)
                    im = weighted[h * 2 * REALS + REALS + b, at, :].astype(F32)
                    wide[b * parts + h, at, :] = re
                    wide[(REALS + b) * parts + h, at, :] = im
                    wide[(2 * REALS + b) * parts + h, at, :] = re + im
                    term = (re * re + im * im) * inverse
                    energy[b] = energy[b] + (term[:8] + term[8:])
    return [
        jnp.sum(jnp.sum(e, axis=0, keepdims=True), axis=1, keepdims=True) for e in energy
    ]


def merge(first, second, width, place):
    low = (place & width) == 0
    other = jnp.where(low, second, first)
    if width == 4:
        other = pltpu.roll(other, 4, 0)
    else:
        other = jnp.where(low, pltpu.roll(other, 8 - width, 0), pltpu.roll(other, width, 0))
    return jnp.where(low, first, second) + other


def site_sums(tiles, wide, sites, reals, block, lanes):
    sums = {}
    parts = tiles.shape[2] // BAND
    for p in range(0, tiles.shape[2], 16):
        h, row = divmod(p, BAND)
        terms = []
        for s in sites:
            tr, ti = (tiles[c, s, pl.ds(p, 16), lanes].astype(F32) for c in range(2))
            terms.append((tr, ti, tr + ti))
        for q in (0, 8):
            at = pl.ds(pl.multiple_of(block * BAND + row + q, 8), 8)
            for b in reals:
                values = [wide[(c * REALS + b) * parts + h, at, :] for c in range(3)]
                for j in range(len(sites)):
                    new = [values[c] * terms[j][c][q : q + 8] for c in range(3)]
                    if (j, b) in sums:
                        new = [x + y for x, y in zip(sums[j, b], new)]
                    sums[j, b] = new
    return {k: (x - y, z - x - y) for k, (x, y, z) in sums.items()}


def synthesize(rows, high, low, energy, stride):
    count, freqs = rows.shape[0], rows.shape[1] // 2
    scaled = rows[...] * frequency_weights(freqs)
    series = product(scaled[:, :freqs], high[:, :freqs], low[:, :freqs]) + product(
        scaled[:, freqs:], high[:, freqs:], low[:, freqs:]
    )
    row = lax.broadcasted_iota(jnp.int32, (count, freqs), 0)
    lane = lane_of((count, freqs))
    carried = jnp.zeros((count, 1), F32)
    index = row[:, 0:1]
    for b in range(REALS):
        hit = (index % stride == b) & (index < 3 * stride)
        carried = jnp.where(hit, energy[b], carried)
    return jnp.where(lane == freqs - 1, carried, series)


def forward_kernel(
    core, weighted, prior, tiles_in, high, low, mine, other, wide, rows, full, tiles, done
):
    sens, points, freqs = tiles.shape[1:]
    fetch = groups_of(tiles_in, tiles, done)
    for k in range(sens // 8):
        fetch(k).start()
    energy = widen(weighted, prior, wide)
    place = lax.broadcasted_iota(jnp.int32, (8, LANES), 0)
    blocks = freqs // LANES

    def part(index, _):
        g = index // blocks
        block = index % blocks
        lanes = pl.ds(pl.multiple_of(block * LANES, LANES), LANES)
        sines = pl.ds(pl.multiple_of(freqs + block * LANES, LANES), LANES)

        @pl.when(block == 0)
        def _():
            fetch(g).wait()

        def pair(k):
            sums = site_sums(tiles, wide, [g * 8 + k, g * 8 + k + 4], range(REALS), block, lanes)
            return [
                [merge(sums[0, b][c], sums[1, b][c], 4, place) for c in range(2)]
                for b in range(REALS)
            ]

        def both(k):
            first = pair(k)
            second = pair(k + 2)
            return [
                [merge(first[b][c], second[b][c], 2, place) for c in range(2)]
                for b in range(REALS)
            ]

        first = both(0)
        second = both(1)
        for b in range(REALS):
            at = pl.ds(pl.multiple_of(b * sens + g * 8, 8), 8)
            rows[at, lanes] = merge(first[b][0], second[b][0], 1, place)
            rows[at, sines] = merge(first[b][1], second[b][1], 1, place)
        return 0

    lax.fori_loop(0, (sens // 8) * blocks, part, 0)
    half = REALS * sens // 2
    series = synthesize(rows, high, low, energy + energy, 8)
    row = lax.broadcasted_iota(jnp.int32, (half, freqs), 0)
    lane = lane_of((half, freqs))
    carried = series[:half, freqs - 1 :]
    full[:half, :] = series[:half]
    full[half:, :] = jnp.where(lane == freqs - 1, carried, series[half:])
    mine[...] = full[pl.ds(pl.multiple_of(core[0] * half, 8), half), :]
    other[...] = full[pl.ds(pl.multiple_of((1 - core[0]) * half, 8), half), :]


def site_kernel(weighted, prior, tiles, high, low, out, wide, rows):
    freqs = tiles.shape[3]
    energy = widen(weighted, prior, wide)
    place = lax.broadcasted_iota(jnp.int32, (8, LANES), 0)

    def part(block, _):
        lanes = pl.ds(pl.multiple_of(block * LANES, LANES), LANES)
        sines = pl.ds(pl.multiple_of(freqs + block * LANES, LANES), LANES)
        for low_b in range(0, REALS, 2):
            sums = site_sums(tiles, wide, range(4), (low_b, low_b + 1), block, lanes)
            for c, where in ((0, lanes), (1, sines)):
                blocks = [sums[j, low_b + b][c] for b in range(2) for j in range(4)]
                for width in (4, 2, 1):
                    half = len(blocks) // 2
                    blocks = [
                        merge(x, y, width, place) for x, y in zip(blocks[:half], blocks[half:])
                    ]
                rows[pl.ds(low_b * 4, 8), where] = blocks[0]
        return 0

    lax.fori_loop(0, freqs // LANES, part, 0)
    out[...] = synthesize(rows, high, low, energy, REALS)


def spread_kernel(mine, got, out, *, stride, begin):
    values = mine[...] + got[...]
    count, freqs = values.shape
    row = lax.broadcasted_iota(jnp.int32, (count, freqs), 0) - begin
    carried = lane_of((count, freqs)) == freqs - 1
    _, second, third = three(values)
    second_row = (row >= stride) & (row < 2 * stride)
    third_row = (row >= 2 * stride) & (row < 3 * stride)
    values = jnp.where(carried & second_row, second, values)
    values = jnp.where(carried & third_row, third, values)
    block = values.astype(BF16)
    for k in range(out.shape[0]):
        out[k] = block


def sum_kernel(got, out):
    total = got[0].astype(F32)
    for k in range(1, got.shape[0]):
        total = total + got[k].astype(F32)
    out[...] = total


def last_kernel(got, begin, later, alpha, series, residual, estimate, predicted):
    reals, sens, steps = estimate.shape
    sites = predicted.shape[1]
    count = reals * sites
    total = got[0].astype(F32)
    for k in range(1, got.shape[0]):
        total = total + got[k].astype(F32)
    last = total.shape[1] - 1
    for b in range(reals):
        rows = [count + k * reals + b for k in range(3)]
        energy = sum(total[r : r + 1, last:] for r in rows)

        def value(ref, kind):
            return ref[0:1, kind * reals + b : kind * reals + b + 1]

        beta = value(later, 0) / value(begin, 0)
        curve = energy + value(later, 1) + 2.0 * beta * value(later, 2)
        curve = curve + beta * beta * value(begin, 1)
        first = value(alpha, 0)
        second = value(later, 0) / curve
        at = slice(b * sens, (b + 1) * sens)
        values = series[at, :]
        result = first * values + second * (residual[at, :] + beta * values)
        estimate[b] = result[:, :steps]
        low = total[b * sites : (b + 1) * sites]
        high = total[count + b * sites : count + (b + 1) * sites]
        predicted[b] = (first * low + second * high)[:, :steps]


def in_hbm(array):
    return pltpu.with_memory_space_constraint(array, pltpu.HBM)


def call(kernel, name, outs, scratch, specs, *args, send=False, semaphores=(), limit=24 * 2**20):
    scratch = [pltpu.VMEM(*one) for one in scratch]
    args = [in_hbm(arg) if spec is HBM else arg for arg, spec in zip(args, specs)]
    scratch += [pltpu.SemaphoreType.DMA((number,)) for number in semaphores]
    return pl.pallas_call(
        kernel,
        in_specs=specs,
        out_specs=[HBM if send and k == 0 else VMEM for k in range(len(outs))],
        out_shape=[jax.ShapeDtypeStruct(*out) for out in outs],
        scratch_shapes=scratch,
        compiler_params=pltpu.CompilerParams(vmem_limit_bytes=limit),
        name=name,
    )(*args)


def on_device(records, tiles, gauges, prior, noise):
    reals, sensors, steps = records.shape
    points, freqs = prior.shape
    sites = gauges.shape[1]
    tables = make_tables(freqs)
    senders = lax.axis_size("y") * lax.axis_size("x")
    heights = lax.axis_size("z")
    place = lax.axis_index("y") * lax.axis_size("x") + lax.axis_index("x")
    core = lax.axis_index("core").astype(jnp.int32).reshape(1)
    start = place // (2 * reals) * BAND
    prior_chunk = lax.dynamic_slice(prior, (start, 0), (BAND, freqs))
    pick = lax.rem(place, reals).astype(jnp.int32).reshape(1)
    count = reals * sensors
    half = count // 2
    block_rows = BAND * freqs // LANES
    message = ((senders, block_rows + EXTRA, LANES), BF16)
    weighted_shape = (senders, block_rows, LANES)
    wide_shape = (3 * senders // 2, block_rows, LANES)
    spectra = ((count, 2 * freqs), F32)
    rows = ((count, freqs), F32)
    tile = ((8, LANES), F32)

    def swap(block):
        return lax.ppermute(block, "core", [(0, 1), (1, 0)])

    bands = points // BAND
    pieces = bands * (sensors // 8)
    local = (tiles.shape, BF16)
    sent, series, noisy, *tables = call(
        first_kernel,
        "first",
        [message, rows, ((sensors, 1), F32)] + [(table.shape, BF16) for table in tables],
        [(records.shape, F32), ((1, sensors), F32), local, spectra, message],
        [HBM] * 5,
        *(records, noise.reshape(1, sensors), tiles, *tables),
        send=True,
        semaphores=[4 + pieces, 7],
    )
    got = lax.all_to_all(sent, SENS, 0, 0)
    sent, points_0, begin = call(
        weigh_kernel,
        "weigh",
        [(weighted_shape, BF16), ((block_rows, LANES), F32), tile],
        [],
        [VMEM] * 2,
        *(got, prior_chunk),
    )
    weighted_0 = lax.all_to_all(sent, SENS, 0, 0)
    mine, other = call(
        forward_kernel,
        "forward",
        [((half, freqs), F32)] * 2,
        [(wide_shape, F32), spectra, rows, local],
        [SMEM, VMEM, VMEM, HBM, VMEM, VMEM],
        *(core, weighted_0, prior, tiles, *tables),
        semaphores=[sensors // 8],
    )
    (sent,) = call(
        functools.partial(spread_kernel, stride=8, begin=0),
        "spread",
        [((heights, half, freqs), BF16)],
        [],
        [VMEM] * 2,
        *(mine, swap(other)),
    )
    got = lax.all_to_all(sent, "z", 0, 0)
    (mine,) = call(sum_kernel, "gather", [((half, freqs), F32)], [], [VMEM], got)
    theirs = swap(mine)
    sent, residual, alpha = call(
        second_kernel,
        "second",
        [message, rows, tile],
        [rows, local, spectra, message],
        [SMEM] + [VMEM] * 5 + [HBM, VMEM, VMEM],
        *(core, mine, theirs, series, noisy, begin, tiles, *tables),
        send=True,
        semaphores=[pieces, 7],
    )
    got = lax.all_to_all(sent, SENS, 0, 0)
    sent, later = call(
        weigh_next_kernel,
        "weigh_next",
        [(weighted_shape, BF16), tile],
        [],
        [VMEM] * 4 + [SMEM],
        *(got, prior_chunk, points_0, begin, pick),
    )
    weighted_1 = lax.all_to_all(sent, SENS, 0, 0)

    def site(weighted, name):
        return call(
            site_kernel,
            name,
            [((reals * sites, freqs), F32)],
            [(wide_shape, F32), ((reals * sites, 2 * freqs), F32)],
            [VMEM] * 5,
            *(weighted, prior, gauges, *tables),
        )[0]

    block = jnp.concatenate([site(weighted_0, "site_0"), site(weighted_1, "site_1")])
    (sent,) = call(
        functools.partial(spread_kernel, stride=reals, begin=reals * sites),
        "spread_sites",
        [((heights,) + block.shape, BF16)],
        [],
        [VMEM] * 2,
        *(block, swap(block)),
    )
    got = lax.all_to_all(sent, "z", 0, 0)
    estimate, predicted = call(
        last_kernel,
        "last",
        [((reals, sensors, steps), F32), ((reals, sites, steps), F32)],
        [],
        [VMEM] * 6,
        *(got, begin, later, alpha, series, residual),
    )
    return (estimate, predicted)


def solution(mesh):
    fine = Mesh(mesh.devices.reshape(4, 4, 8, 2), SENS + PTS)
    return jax.shard_map(
        on_device,
        mesh=fine,
        in_specs=(
            P(None, SENS, None),
            P(None, SENS, PTS, None),
            P(None, SENS, PTS, None),
            P(PTS, None),
            P(SENS),
        ),
        out_specs=(P(None, SENS, None), P(None, SENS, None)),
        check_vma=False,
    )
```

```python
import functools

import jax
import jax.numpy as jnp
import numpy as np
from jax import lax
from jax.experimental import pallas as pl
from jax.experimental.pallas import tpu as pltpu
from jax.sharding import Mesh
from jax.sharding import PartitionSpec as P

SENS = ("y", "x")
PTS = ("z", "core")
REALS = 4
LANES = 128
BAND = 32
EXTRA = 16
F32 = jnp.float32
BF16 = jnp.bfloat16
VMEM = pl.BlockSpec(memory_space=pltpu.VMEM)
HBM = pl.BlockSpec(memory_space=pltpu.HBM)
SMEM = pl.BlockSpec(memory_space=pltpu.SMEM)


def make_tables(freqs):
    padded = 2 * (freqs - 1)
    steps = np.arange(freqs, dtype=np.int64)
    angle = (steps[:, None] * steps[None, :] % padded) * (2.0 * np.pi / padded)
    both = np.concatenate([np.cos(angle), -np.sin(angle)], axis=1)
    high = both.astype(BF16)
    low = (both - high.astype(np.float64)).astype(BF16)
    return jnp.asarray(high), jnp.asarray(low)


def frequency_weights(freqs):
    at = lax.broadcasted_iota(jnp.int32, (1, 2 * freqs), 1)
    at = jnp.where(at < freqs, at, at - freqs)
    padded = 2 * (freqs - 1)
    return jnp.where((at == 0) | (at == freqs - 1), 1.0 / padded, 2.0 / padded)


def product(left, high, low):
    first = left.astype(BF16)
    second = (left - first.astype(F32)).astype(BF16)

    def dot(a, b):
        return jnp.dot(a, b, preferred_element_type=F32)

    return dot(first, high) + (dot(first, low) + dot(second, high))


def lane_of(shape):
    return lax.broadcasted_iota(jnp.int32, shape, len(shape) - 1)


def three(values):
    first = values.astype(BF16).astype(F32)
    rest = values - first
    second = rest.astype(BF16).astype(F32)
    return first, second, rest - second


def write_scalars(out, columns):
    lane = lane_of((8, LANES))
    tile = jnp.zeros((8, LANES), F32)
    for k, column in enumerate(columns):
        tile = jnp.where(lane == k, column, tile)
    first, second, third = three(tile)
    tile = first + pltpu.roll(second, 32, 1) + pltpu.roll(third, 64, 1)
    block = jnp.concatenate([tile, jnp.zeros_like(tile)]).astype(BF16)
    rows = out.shape[1] - EXTRA
    for k in range(out.shape[0]):
        out[k, rows:, :] = block


def band_sum(first, second, start, count):
    total = jnp.zeros((8, first.shape[1]), F32)
    for row in range(start, start + count, 8):
        total = total + first[row : row + 8, :] * second[row : row + 8, :]
    return jnp.sum(total, axis=1, keepdims=True)


def pieces_of(source, target, done, first=0):
    groups = source.shape[1] // 8

    def copy(band, group):
        at = (slice(None), pl.ds(group * 8, 8), pl.ds(pl.multiple_of(band * BAND, BAND), BAND))
        return pltpu.make_async_copy(
            source.at[at], target.at[at], done.at[first + band * groups + group]
        )

    copies = [copy(b, g) for b in range(source.shape[2] // BAND) for g in range(groups)]
    return copy, copies


def groups_of(source, target, done):
    def copy(group):
        at = pl.ds(group * 8, 8)
        return pltpu.make_async_copy(source.at[:, at], target.at[:, at], done.at[group])

    return copy


def send_points(series, tiles, copy, high, low, spec, out):
    sens, points, freqs = tiles.shape[1:]
    spec[...] = product(series[...], high[...], low[...]) * frequency_weights(freqs)
    blocks = freqs // LANES

    def part(index, _):
        band = index // blocks
        block = index % blocks
        lanes = pl.ds(pl.multiple_of(block * LANES, LANES), LANES)
        sines = pl.ds(pl.multiple_of(freqs + block * LANES, LANES), LANES)
        range_ = pl.ds(pl.multiple_of(band * BAND, BAND), BAND)

        def group(g, acc):
            @pl.when(block == 0)
            def _():
                copy(band, g).wait()

            acc = list(acc)
            rows = [pl.ds(pl.multiple_of(b * sens + g * 8, 8), 8) for b in range(REALS)]
            real = [spec[r, lanes] for r in rows]
            imag = [spec[r, sines] for r in rows]
            for j in range(8):
                tr = tiles[0, g * 8 + j, range_, lanes].astype(F32)
                ti = tiles[1, g * 8 + j, range_, lanes].astype(F32)
                for b in range(REALS):
                    sr = real[b][j : j + 1]
                    si = imag[b][j : j + 1]
                    re, im = acc[b]
                    acc[b] = (re + (sr * tr + si * ti), im + (si * tr - sr * ti))
            return tuple(acc)

        zero = jnp.zeros((BAND, LANES), F32)
        acc = lax.fori_loop(0, sens // 8, group, ((zero, zero),) * REALS)
        rows = pl.ds(pl.multiple_of(block * BAND, BAND), BAND)
        for b in range(REALS):
            for c in range(2):
                out[band * 2 * REALS + c * REALS + b, rows, :] = acc[b][c].astype(BF16)
        return 0

    lax.fori_loop(0, (points // BAND) * blocks, part, 0)


def first_kernel(
    records, noise, tiles_in, high_in, low_in, out, series, column, high, low, raw, raw_noise, tiles, spec, done
):
    reals, sens, steps = records.shape
    moves = ((records, raw), (noise, raw_noise), (high_in, high), (low_in, low))
    copies = [pltpu.make_async_copy(*move, done.at[k]) for k, move in enumerate(moves)]
    fetch, pieces = pieces_of(tiles_in, tiles, done, len(copies))
    for copy in copies + pieces:
        copy.start()
    copies[0].wait()
    copies[1].wait()
    row = lax.broadcasted_iota(jnp.int32, (sens, sens), 0)
    noises = jnp.where(row == lane_of((sens, sens)), raw_noise[...], 0.0)
    noises = jnp.sum(noises, axis=1, keepdims=True)
    column[...] = noises
    series[...] = jnp.zeros_like(series)
    columns = [[], []]
    for b in range(reals):
        series[b * sens : (b + 1) * sens, :steps] = raw[b]
    for b in range(reals):
        values = series[b * sens : (b + 1) * sens, :]
        columns[0].append(band_sum(values, values, 0, sens))
        columns[1].append(band_sum(values, values * noises, 0, sens))
    write_scalars(out, columns[0] + columns[1])
    copies[2].wait()
    copies[3].wait()
    send_points(series, tiles, fetch, high, low, spec, out)


def second_kernel(
    core, mine, theirs, series, noise, begin, tiles_in, high, low, out, residual, alpha, image, tiles, spec, done
):
    fetch, pieces = pieces_of(tiles_in, tiles, done)
    for copy in pieces:
        copy.start()
    half, freqs = mine.shape
    sens = 2 * half // REALS
    image[pl.ds(pl.multiple_of(core[0] * half, 8), half), :] = mine[...]
    image[pl.ds(pl.multiple_of((1 - core[0]) * half, 8), half), :] = theirs[...]
    lane = lane_of((8, LANES))
    tile = jnp.zeros((8, LANES), F32)
    real = lane_of((sens, freqs)) < freqs - 1
    last = freqs - 1
    columns = [[], [], []]
    for b in range(REALS):
        energy = image[b : b + 1, last:] + image[8 + b : 9 + b, last:] + image[16 + b : 17 + b, last:]
        scale = begin[0:1, b : b + 1] / (energy + begin[0:1, REALS + b : REALS + b + 1])
        tile = jnp.where(lane == b, scale, tile)
        rows = slice(b * sens, (b + 1) * sens)
        values = series[rows, :]
        noisy = noise[...]
        left = values - scale * (jnp.where(real, image[rows, :], 0.0) + noisy * values)
        residual[rows, :] = left
        columns[0].append(band_sum(left, left, 0, sens))
        columns[1].append(band_sum(left, left * noisy, 0, sens))
        columns[2].append(band_sum(left, values * noisy, 0, sens))
    alpha[...] = tile
    write_scalars(out, columns[0] + columns[1] + columns[2])
    send_points(residual, tiles, fetch, high, low, spec, out)


def sum_message(got):
    rows = got.shape[1] - EXTRA
    total = got[0, :rows, :].astype(F32)
    extra = got[0, rows:, :].astype(F32)
    for k in range(1, got.shape[0]):
        total = total + got[k, :rows, :].astype(F32)
        extra = extra + got[k, rows:, :].astype(F32)
    sums = jnp.broadcast_to(jnp.sum(extra, axis=0, keepdims=True), (8, LANES))
    sums = sums + pltpu.roll(sums, LANES - 32, 1) + pltpu.roll(sums, LANES - 64, 1)
    return total, sums


def put_weighted(total, prior, start, out):
    points = pl.ds(pl.multiple_of(start[0], BAND), BAND)
    for block in range(prior.shape[1] // LANES):
        rows = slice(block * BAND, (block + 1) * BAND)
        lanes = slice(block * LANES, (block + 1) * LANES)
        part = (total[rows] * prior[points, lanes]).astype(BF16)
        for k in range(out.shape[0]):
            out[k, rows, :] = part


def weigh_kernel(got, prior, start, out, kept, sums_out):
    total, sums = sum_message(got)
    kept[...] = total
    sums_out[...] = sums
    put_weighted(total, prior, start, out)


def weigh_next_kernel(got, prior, before, begin, pick, start, out, sums_out):
    total, sums = sum_message(got)
    sums_out[...] = sums
    lane = lane_of((8, LANES))
    ratio = sums / jnp.where(lane < REALS, begin[...], 1.0)
    beta = jnp.sum(jnp.where(lane == pick[0], ratio, 0.0), axis=1, keepdims=True)[0:1]
    put_weighted(total + beta * before[...], prior, start, out)


def widen(weighted, prior, wide):
    energy = [jnp.zeros((8, LANES), F32)] * REALS
    parts = weighted.shape[0] // (2 * REALS)
    for h in range(parts):
        for block in range(prior.shape[1] // LANES):
            for row in range(0, BAND, 16):
                lanes = slice(block * LANES, (block + 1) * LANES)
                inverse = 1.0 / prior[h * BAND + row : h * BAND + row + 16, lanes]
                for b in range(REALS):
                    at = slice(block * BAND + row, block * BAND + row + 16)
                    re = weighted[h * 2 * REALS + b, at, :].astype(F32)
                    im = weighted[h * 2 * REALS + REALS + b, at, :].astype(F32)
                    wide[b * parts + h, at, :] = re
                    wide[(REALS + b) * parts + h, at, :] = im
                    wide[(2 * REALS + b) * parts + h, at, :] = re + im
                    term = (re * re + im * im) * inverse
                    energy[b] = energy[b] + (term[:8] + term[8:])
    return [
        jnp.sum(jnp.sum(e, axis=0, keepdims=True), axis=1, keepdims=True) for e in energy
    ]


def merge(first, second, width, place):
    low = (place & width) == 0
    other = jnp.where(low, second, first)
    if width == 4:
        other = pltpu.roll(other, 4, 0)
    else:
        other = jnp.where(low, pltpu.roll(other, 8 - width, 0), pltpu.roll(other, width, 0))
    return jnp.where(low, first, second) + other


def site_sums(tiles, wide, sites, reals, block, lanes):
    sums = {}
    parts = tiles.shape[2] // BAND
    for p in range(0, tiles.shape[2], 16):
        h, row = divmod(p, BAND)
        terms = []
        for s in sites:
            tr, ti = (tiles[c, s, pl.ds(p, 16), lanes].astype(F32) for c in range(2))
            terms.append((tr, ti, tr + ti))
        for q in (0, 8):
            at = pl.ds(pl.multiple_of(block * BAND + row + q, 8), 8)
            for b in reals:
                values = [wide[(c * REALS + b) * parts + h, at, :] for c in range(3)]
                for j in range(len(sites)):
                    new = [values[c] * terms[j][c][q : q + 8] for c in range(3)]
                    if (j, b) in sums:
                        new = [x + y for x, y in zip(sums[j, b], new)]
                    sums[j, b] = new
    return {k: (x - y, z - x - y) for k, (x, y, z) in sums.items()}


def synthesize(rows, high, low, energy, stride):
    count, freqs = rows.shape[0], rows.shape[1] // 2
    scaled = rows[...] * frequency_weights(freqs)
    series = product(scaled[:, :freqs], high[:, :freqs], low[:, :freqs]) + product(
        scaled[:, freqs:], high[:, freqs:], low[:, freqs:]
    )
    row = lax.broadcasted_iota(jnp.int32, (count, freqs), 0)
    lane = lane_of((count, freqs))
    carried = jnp.zeros((count, 1), F32)
    index = row[:, 0:1]
    for b in range(REALS):
        hit = (index % stride == b) & (index < 3 * stride)
        carried = jnp.where(hit, energy[b], carried)
    return jnp.where(lane == freqs - 1, carried, series)


def forward_kernel(
    core, weighted, prior, tiles_in, high, low, mine, other, wide, rows, full, tiles, done
):
    sens, points, freqs = tiles.shape[1:]
    fetch = groups_of(tiles_in, tiles, done)
    for k in range(sens // 8):
        fetch(k).start()
    energy = widen(weighted, prior, wide)
    place = lax.broadcasted_iota(jnp.int32, (8, LANES), 0)
    blocks = freqs // LANES

    def part(index, _):
        g = index // blocks
        block = index % blocks
        lanes = pl.ds(pl.multiple_of(block * LANES, LANES), LANES)
        sines = pl.ds(pl.multiple_of(freqs + block * LANES, LANES), LANES)

        @pl.when(block == 0)
        def _():
            fetch(g).wait()

        def pair(k):
            sums = site_sums(tiles, wide, [g * 8 + k, g * 8 + k + 4], range(REALS), block, lanes)
            return [
                [merge(sums[0, b][c], sums[1, b][c], 4, place) for c in range(2)]
                for b in range(REALS)
            ]

        def both(k):
            first = pair(k)
            second = pair(k + 2)
            return [
                [merge(first[b][c], second[b][c], 2, place) for c in range(2)]
                for b in range(REALS)
            ]

        first = both(0)
        second = both(1)
        for b in range(REALS):
            at = pl.ds(pl.multiple_of(b * sens + g * 8, 8), 8)
            rows[at, lanes] = merge(first[b][0], second[b][0], 1, place)
            rows[at, sines] = merge(first[b][1], second[b][1], 1, place)
        return 0

    lax.fori_loop(0, (sens // 8) * blocks, part, 0)
    half = REALS * sens // 2
    series = synthesize(rows, high, low, energy + energy, 8)
    row = lax.broadcasted_iota(jnp.int32, (half, freqs), 0)
    lane = lane_of((half, freqs))
    carried = series[:half, freqs - 1 :]
    full[:half, :] = series[:half]
    full[half:, :] = jnp.where(lane == freqs - 1, carried, series[half:])
    mine[...] = full[pl.ds(pl.multiple_of(core[0] * half, 8), half), :]
    other[...] = full[pl.ds(pl.multiple_of((1 - core[0]) * half, 8), half), :]


def site_kernel(weighted, prior, tiles, high, low, out, wide, rows):
    freqs = tiles.shape[3]
    energy = widen(weighted, prior, wide)
    place = lax.broadcasted_iota(jnp.int32, (8, LANES), 0)

    def part(block, _):
        lanes = pl.ds(pl.multiple_of(block * LANES, LANES), LANES)
        sines = pl.ds(pl.multiple_of(freqs + block * LANES, LANES), LANES)
        for low_b in range(0, REALS, 2):
            sums = site_sums(tiles, wide, range(4), (low_b, low_b + 1), block, lanes)
            for c, where in ((0, lanes), (1, sines)):
                blocks = [sums[j, low_b + b][c] for b in range(2) for j in range(4)]
                for width in (4, 2, 1):
                    half = len(blocks) // 2
                    blocks = [
                        merge(x, y, width, place) for x, y in zip(blocks[:half], blocks[half:])
                    ]
                rows[pl.ds(low_b * 4, 8), where] = blocks[0]
        return 0

    lax.fori_loop(0, freqs // LANES, part, 0)
    out[...] = synthesize(rows, high, low, energy, REALS)


def spread_kernel(mine, got, out, *, stride, begin):
    values = mine[...] + got[...]
    count, freqs = values.shape
    row = lax.broadcasted_iota(jnp.int32, (count, freqs), 0) - begin
    carried = lane_of((count, freqs)) == freqs - 1
    _, second, third = three(values)
    second_row = (row >= stride) & (row < 2 * stride)
    third_row = (row >= 2 * stride) & (row < 3 * stride)
    values = jnp.where(carried & second_row, second, values)
    values = jnp.where(carried & third_row, third, values)
    block = values.astype(BF16)
    for k in range(out.shape[0]):
        out[k] = block


def sum_kernel(got, out):
    total = got[0].astype(F32)
    for k in range(1, got.shape[0]):
        total = total + got[k].astype(F32)
    out[...] = total


def last_kernel(got, begin, later, alpha, series, residual, estimate, predicted):
    reals, sens, steps = estimate.shape
    sites = predicted.shape[1]
    count = reals * sites
    total = got[0].astype(F32)
    for k in range(1, got.shape[0]):
        total = total + got[k].astype(F32)
    last = total.shape[1] - 1
    for b in range(reals):
        rows = [count + k * reals + b for k in range(3)]
        energy = sum(total[r : r + 1, last:] for r in rows)

        def value(ref, kind):
            return ref[0:1, kind * reals + b : kind * reals + b + 1]

        beta = value(later, 0) / value(begin, 0)
        curve = energy + value(later, 1) + 2.0 * beta * value(later, 2)
        curve = curve + beta * beta * value(begin, 1)
        first = value(alpha, 0)
        second = value(later, 0) / curve
        at = slice(b * sens, (b + 1) * sens)
        values = series[at, :]
        result = first * values + second * (residual[at, :] + beta * values)
        estimate[b] = result[:, :steps]
        low = total[b * sites : (b + 1) * sites]
        high = total[count + b * sites : count + (b + 1) * sites]
        predicted[b] = (first * low + second * high)[:, :steps]


def in_hbm(array):
    return pltpu.with_memory_space_constraint(array, pltpu.HBM)


def call(kernel, name, outs, scratch, specs, *args, semaphores=(), limit=24 * 2**20):
    scratch = [pltpu.VMEM(*one) for one in scratch]
    args = [in_hbm(arg) if spec is HBM else arg for arg, spec in zip(args, specs)]
    scratch += [pltpu.SemaphoreType.DMA((number,)) for number in semaphores]
    return pl.pallas_call(
        kernel,
        in_specs=specs,
        out_specs=[VMEM] * len(outs),
        out_shape=[jax.ShapeDtypeStruct(*out) for out in outs],
        scratch_shapes=scratch,
        compiler_params=pltpu.CompilerParams(vmem_limit_bytes=limit),
        name=name,
    )(*args)


def on_device(records, tiles, gauges, prior, noise):
    reals, sensors, steps = records.shape
    points, freqs = prior.shape
    sites = gauges.shape[1]
    tables = make_tables(freqs)
    senders = lax.axis_size("y") * lax.axis_size("x")
    heights = lax.axis_size("z")
    place = lax.axis_index("y") * lax.axis_size("x") + lax.axis_index("x")
    core = lax.axis_index("core").astype(jnp.int32).reshape(1)
    start = (place // (2 * reals) * BAND).astype(jnp.int32).reshape(1)
    pick = lax.rem(place, reals).astype(jnp.int32).reshape(1)
    core, pick, start, prior, gauges, records = lax.optimization_barrier(
        (core, pick, start, prior, gauges, records)
    )
    count = reals * sensors
    half = count // 2
    block_rows = BAND * freqs // LANES
    message = ((senders, block_rows + EXTRA, LANES), BF16)
    weighted_shape = (senders, block_rows, LANES)
    wide_shape = (3 * senders // 2, block_rows, LANES)
    spectra = ((count, 2 * freqs), F32)
    rows = ((count, freqs), F32)
    tile = ((8, LANES), F32)

    def swap(block):
        return lax.ppermute(block, "core", [(0, 1), (1, 0)])

    def site(weighted, name, tables):
        return call(
            site_kernel,
            name,
            [((reals * sites, freqs), F32)],
            [(wide_shape, F32), ((reals * sites, 2 * freqs), F32)],
            [VMEM] * 5,
            *(weighted, prior, gauges, *tables),
        )[0]

    bands = points // BAND
    pieces = bands * (sensors // 8)
    local = (tiles.shape, BF16)
    sent, series, noisy, *tables = call(
        first_kernel,
        "first",
        [message, rows, ((sensors, 1), F32)] + [(table.shape, BF16) for table in tables],
        [(records.shape, F32), ((1, sensors), F32), local, spectra],
        [HBM] * 5,
        *(records, noise.reshape(1, sensors), tiles, *tables),
        semaphores=[4 + pieces],
    )
    got = lax.all_to_all(sent, SENS, 0, 0)
    sent, points_0, begin = call(
        weigh_kernel,
        "weigh",
        [(weighted_shape, BF16), ((block_rows, LANES), F32), tile],
        [],
        [VMEM, VMEM, SMEM],
        *(got, prior, start),
    )
    weighted_0 = lax.all_to_all(sent, SENS, 0, 0)
    mine, other = call(
        forward_kernel,
        "forward",
        [((half, freqs), F32)] * 2,
        [(wide_shape, F32), spectra, rows, local],
        [SMEM, VMEM, VMEM, HBM, VMEM, VMEM],
        *(core, weighted_0, prior, tiles, *tables),
        semaphores=[sensors // 8],
    )
    (sent,) = call(
        functools.partial(spread_kernel, stride=8, begin=0),
        "spread",
        [((heights, half, freqs), BF16)],
        [],
        [VMEM] * 2,
        *(mine, swap(other)),
    )
    got = lax.all_to_all(sent, "z", 0, 0)
    (mine,) = call(sum_kernel, "gather", [((half, freqs), F32)], [], [VMEM], got)
    weighted_0, mine = lax.optimization_barrier((weighted_0, mine))
    site_0 = site(weighted_0, "site_0", tables)
    theirs, site_0 = lax.optimization_barrier((swap(mine), site_0))
    sent, residual, alpha = call(
        second_kernel,
        "second",
        [message, rows, tile],
        [rows, local, spectra],
        [SMEM] + [VMEM] * 5 + [HBM, VMEM, VMEM],
        *(core, mine, theirs, series, noisy, begin, tiles, *tables),
        semaphores=[pieces],
    )
    got = lax.all_to_all(sent, SENS, 0, 0)
    sent, later = call(
        weigh_next_kernel,
        "weigh_next",
        [(weighted_shape, BF16), tile],
        [],
        [VMEM] * 4 + [SMEM] * 2,
        *(got, prior, points_0, begin, pick, start),
    )
    weighted_1 = lax.all_to_all(sent, SENS, 0, 0)

    block = jnp.concatenate([site_0, site(weighted_1, "site_1", tables)])
    (sent,) = call(
        functools.partial(spread_kernel, stride=reals, begin=reals * sites),
        "spread_sites",
        [((heights,) + block.shape, BF16)],
        [],
        [VMEM] * 2,
        *(block, swap(block)),
    )
    got = lax.all_to_all(sent, "z", 0, 0)
    estimate, predicted = call(
        last_kernel,
        "last",
        [((reals, sensors, steps), F32), ((reals, sites, steps), F32)],
        [],
        [VMEM] * 6,
        *(got, begin, later, alpha, series, residual),
    )
    return (estimate, predicted)


def solution(mesh):
    fine = Mesh(mesh.devices.reshape(4, 4, 8, 2), SENS + PTS)
    return jax.shard_map(
        on_device,
        mesh=fine,
        in_specs=(
            P(None, SENS, None),
            P(None, SENS, PTS, None),
            P(None, SENS, PTS, None),
            P(PTS, None),
            P(SENS),
        ),
        out_specs=(P(None, SENS, None), P(None, SENS, None)),
        check_vma=False,
    )
```

```python
import functools

import jax
import jax.numpy as jnp
import numpy as np
from jax import lax
from jax.experimental import pallas as pl
from jax.experimental.pallas import tpu as pltpu
from jax.sharding import Mesh
from jax.sharding import PartitionSpec as P

SENS = ("y", "x")
PTS = ("z", "core")
REALS = 4
LANES = 128
BAND = 32
EXTRA = 8
F32 = jnp.float32
BF16 = jnp.bfloat16
VMEM = pl.BlockSpec(memory_space=pltpu.VMEM)
HBM = pl.BlockSpec(memory_space=pltpu.HBM)
SMEM = pl.BlockSpec(memory_space=pltpu.SMEM)


def make_tables(freqs):
    padded = 2 * (freqs - 1)
    steps = np.arange(freqs, dtype=np.int64)
    angle = (steps[:, None] * steps[None, :] % padded) * (2.0 * np.pi / padded)
    both = np.concatenate([np.cos(angle), -np.sin(angle)], axis=1)
    high = both.astype(BF16)
    low = (both - high.astype(np.float64)).astype(BF16)
    return jnp.asarray(high), jnp.asarray(low)


def frequency_weights(freqs):
    at = lax.broadcasted_iota(jnp.int32, (1, 2 * freqs), 1)
    at = jnp.where(at < freqs, at, at - freqs)
    padded = 2 * (freqs - 1)
    return jnp.where((at == 0) | (at == freqs - 1), 1.0 / padded, 2.0 / padded)


def product(left, high, low):
    first = left.astype(BF16)
    second = (left - first.astype(F32)).astype(BF16)

    def dot(a, b):
        return jnp.dot(a, b, preferred_element_type=F32)

    return dot(first, high) + (dot(first, low) + dot(second, high))


def lane_of(shape):
    return lax.broadcasted_iota(jnp.int32, shape, len(shape) - 1)


def three(values):
    first = values.astype(BF16).astype(F32)
    rest = values - first
    second = rest.astype(BF16).astype(F32)
    return first, second, rest - second


def write_scalars(out, columns):
    lane = lane_of((8, LANES))
    tile = jnp.zeros((8, LANES), F32)
    for k, column in enumerate(columns):
        tile = jnp.where(lane == k, column, tile)
    first, second, third = three(tile)
    tile = first + pltpu.roll(second, 32, 1) + pltpu.roll(third, 64, 1)
    block = tile.astype(BF16)
    rows = out.shape[1] - EXTRA
    for k in range(out.shape[0]):
        out[k, rows:, :] = block


def band_sum(first, second, start, count):
    total = jnp.zeros((8, first.shape[1]), F32)
    for row in range(start, start + count, 8):
        total = total + first[row : row + 8, :] * second[row : row + 8, :]
    return jnp.sum(total, axis=1, keepdims=True)


def pieces_of(source, target, done, first=0):
    groups = source.shape[1] // 8

    def copy(band, group):
        at = (slice(None), pl.ds(group * 8, 8), pl.ds(pl.multiple_of(band * BAND, BAND), BAND))
        return pltpu.make_async_copy(
            source.at[at], target.at[at], done.at[first + band * groups + group]
        )

    copies = [copy(b, g) for b in range(source.shape[2] // BAND) for g in range(groups)]
    return copy, copies


def groups_of(source, target, done):
    def copy(group):
        at = pl.ds(group * 8, 8)
        return pltpu.make_async_copy(source.at[:, at], target.at[:, at], done.at[group])

    return copy


def send_points(series, tiles, copy, high, low, spec, out):
    sens, points, freqs = tiles.shape[1:]
    pair = product(series[...], high[...], low[...]) * frequency_weights(freqs)
    spec[...] = pair.reshape(spec.shape)
    blocks = freqs // LANES

    def part(index, _):
        band = index // blocks
        block = index % blocks
        lanes = pl.ds(pl.multiple_of(block * LANES, LANES), LANES)
        sines = pl.ds(pl.multiple_of(freqs + block * LANES, LANES), LANES)
        range_ = pl.ds(pl.multiple_of(band * BAND, BAND), BAND)

        def group(g, acc):
            @pl.when(block == 0)
            def _():
                copy(band, g).wait()

            acc = list(acc)
            rows = [b * (sens // 8) + g for b in range(REALS)]
            for j in range(8):
                tr = tiles[0, g * 8 + j, range_, lanes].astype(F32)
                ti = tiles[1, g * 8 + j, range_, lanes].astype(F32)
                for b in range(REALS):
                    sr = spec[rows[b], j : j + 1, lanes]
                    si = spec[rows[b], j : j + 1, sines]
                    re, im = acc[b]
                    acc[b] = (re + (sr * tr + si * ti), im + (si * tr - sr * ti))
            return tuple(acc)

        zero = jnp.zeros((BAND, LANES), F32)
        acc = lax.fori_loop(0, sens // 8, group, ((zero, zero),) * REALS)
        rows = pl.ds(pl.multiple_of(block * BAND, BAND), BAND)
        for b in range(REALS):
            for c in range(2):
                out[band * 2 * REALS + c * REALS + b, rows, :] = acc[b][c].astype(BF16)
        return 0

    lax.fori_loop(0, (points // BAND) * blocks, part, 0)


def first_kernel(
    records, noise, tiles_in, high_in, low_in, out, series, column, high, low, raw, raw_noise, tiles, spec, done
):
    reals, sens, steps = records.shape
    moves = ((records, raw), (noise, raw_noise), (high_in, high), (low_in, low))
    copies = [pltpu.make_async_copy(*move, done.at[k]) for k, move in enumerate(moves)]
    fetch, pieces = pieces_of(tiles_in, tiles, done, len(copies))
    for copy in copies + pieces:
        copy.start()
    copies[0].wait()
    copies[1].wait()
    row = lax.broadcasted_iota(jnp.int32, (sens, sens), 0)
    noises = jnp.where(row == lane_of((sens, sens)), raw_noise[...], 0.0)
    noises = jnp.sum(noises, axis=1, keepdims=True)
    column[...] = noises
    series[...] = jnp.zeros_like(series)
    columns = [[], []]
    for b in range(reals):
        series[b * sens : (b + 1) * sens, :steps] = raw[b]
    for b in range(reals):
        values = series[b * sens : (b + 1) * sens, :]
        columns[0].append(band_sum(values, values, 0, sens))
        columns[1].append(band_sum(values, values * noises, 0, sens))
    write_scalars(out, columns[0] + columns[1])
    copies[2].wait()
    copies[3].wait()
    send_points(series, tiles, fetch, high, low, spec, out)


def second_kernel(
    core, mine, theirs, series, noise, begin, tiles_in, high, low, out, residual, alpha, image, tiles, spec, done
):
    fetch, pieces = pieces_of(tiles_in, tiles, done)
    for copy in pieces:
        copy.start()
    half, freqs = mine.shape
    sens = 2 * half // REALS
    image[pl.ds(pl.multiple_of(core[0] * half, 8), half), :] = mine[...]
    image[pl.ds(pl.multiple_of((1 - core[0]) * half, 8), half), :] = theirs[...]
    lane = lane_of((8, LANES))
    tile = jnp.zeros((8, LANES), F32)
    real = lane_of((sens, freqs)) < freqs - 1
    last = freqs - 1
    columns = [[], [], []]
    for b in range(REALS):
        energy = image[b : b + 1, last:] + image[8 + b : 9 + b, last:] + image[16 + b : 17 + b, last:]
        scale = begin[0:1, b : b + 1] / (energy + begin[0:1, REALS + b : REALS + b + 1])
        tile = jnp.where(lane == b, scale, tile)
        rows = slice(b * sens, (b + 1) * sens)
        values = series[rows, :]
        noisy = noise[...]
        left = values - scale * (jnp.where(real, image[rows, :], 0.0) + noisy * values)
        residual[rows, :] = left
        columns[0].append(band_sum(left, left, 0, sens))
        columns[1].append(band_sum(left, left * noisy, 0, sens))
        columns[2].append(band_sum(left, values * noisy, 0, sens))
    alpha[...] = tile
    write_scalars(out, columns[0] + columns[1] + columns[2])
    send_points(residual, tiles, fetch, high, low, spec, out)


def sum_message(got):
    rows = got.shape[1] - EXTRA
    total = got[0, :rows, :].astype(F32)
    extra = got[0, rows:, :].astype(F32)
    for k in range(1, got.shape[0]):
        total = total + got[k, :rows, :].astype(F32)
        extra = extra + got[k, rows:, :].astype(F32)
    sums = jnp.broadcast_to(jnp.sum(extra, axis=0, keepdims=True), (8, LANES))
    sums = sums + pltpu.roll(sums, LANES - 32, 1) + pltpu.roll(sums, LANES - 64, 1)
    return total, sums


def put_weighted(total, prior, start, out):
    points = pl.ds(pl.multiple_of(start[0], BAND), BAND)
    for block in range(prior.shape[1] // LANES):
        rows = slice(block * BAND, (block + 1) * BAND)
        lanes = slice(block * LANES, (block + 1) * LANES)
        part = (total[rows] * prior[points, lanes]).astype(BF16)
        for k in range(out.shape[0]):
            out[k, rows, :] = part


def weigh_kernel(got, prior, start, out, kept, sums_out):
    total, sums = sum_message(got)
    kept[...] = total
    sums_out[...] = sums
    put_weighted(total, prior, start, out)


def weigh_next_kernel(got, prior, before, begin, pick, start, out, sums_out):
    total, sums = sum_message(got)
    sums_out[...] = sums
    lane = lane_of((8, LANES))
    ratio = sums / jnp.where(lane < REALS, begin[...], 1.0)
    beta = jnp.sum(jnp.where(lane == pick[0], ratio, 0.0), axis=1, keepdims=True)[0:1]
    put_weighted(total + beta * before[...], prior, start, out)


def widen(weighted, prior, wide):
    energy = [jnp.zeros((8, LANES), F32)] * REALS
    parts = weighted.shape[0] // (2 * REALS)
    for h in range(parts):
        for block in range(prior.shape[1] // LANES):
            for row in range(0, BAND, 16):
                lanes = slice(block * LANES, (block + 1) * LANES)
                inverse = 1.0 / prior[h * BAND + row : h * BAND + row + 16, lanes]
                for b in range(REALS):
                    at = slice(block * BAND + row, block * BAND + row + 16)
                    re = weighted[h * 2 * REALS + b, at, :].astype(F32)
                    im = weighted[h * 2 * REALS + REALS + b, at, :].astype(F32)
                    wide[b * parts + h, at, :] = re
                    wide[(REALS + b) * parts + h, at, :] = im
                    wide[(2 * REALS + b) * parts + h, at, :] = re + im
                    term = (re * re + im * im) * inverse
                    energy[b] = energy[b] + (term[:8] + term[8:])
    return [
        jnp.sum(jnp.sum(e, axis=0, keepdims=True), axis=1, keepdims=True) for e in energy
    ]


def merge(first, second, width, place):
    low = (place & width) == 0
    other = jnp.where(low, second, first)
    if width == 4:
        other = pltpu.roll(other, 4, 0)
    else:
        other = jnp.where(low, pltpu.roll(other, 8 - width, 0), pltpu.roll(other, width, 0))
    return jnp.where(low, first, second) + other


def site_sums(tiles, wide, sites, reals, block, lanes):
    sums = {}
    parts = tiles.shape[2] // BAND
    for p in range(0, tiles.shape[2], 16):
        h, row = divmod(p, BAND)
        terms = []
        for s in sites:
            tr, ti = (tiles[c, s, pl.ds(p, 16), lanes].astype(F32) for c in range(2))
            terms.append((tr, ti, tr + ti))
        for q in (0, 8):
            at = pl.ds(pl.multiple_of(block * BAND + row + q, 8), 8)
            for b in reals:
                values = [wide[(c * REALS + b) * parts + h, at, :] for c in range(3)]
                for j in range(len(sites)):
                    new = [values[c] * terms[j][c][q : q + 8] for c in range(3)]
                    if (j, b) in sums:
                        new = [x + y for x, y in zip(sums[j, b], new)]
                    sums[j, b] = new
    return {k: (x - y, z - x - y) for k, (x, y, z) in sums.items()}


def synthesize(rows, high, low, energy, stride):
    count, freqs = rows.shape[0], rows.shape[1] // 2
    scaled = rows[...] * frequency_weights(freqs)
    series = product(scaled[:, :freqs], high[:, :freqs], low[:, :freqs]) + product(
        scaled[:, freqs:], high[:, freqs:], low[:, freqs:]
    )
    row = lax.broadcasted_iota(jnp.int32, (count, freqs), 0)
    lane = lane_of((count, freqs))
    carried = jnp.zeros((count, 1), F32)
    index = row[:, 0:1]
    for b in range(REALS):
        hit = (index % stride == b) & (index < 3 * stride)
        carried = jnp.where(hit, energy[b], carried)
    return jnp.where(lane == freqs - 1, carried, series)


def forward_kernel(
    core, weighted, prior, tiles_in, high, low, mine, other, wide, rows, full, tiles, done
):
    sens, points, freqs = tiles.shape[1:]
    fetch = groups_of(tiles_in, tiles, done)
    for k in range(sens // 8):
        fetch(k).start()
    energy = widen(weighted, prior, wide)
    place = lax.broadcasted_iota(jnp.int32, (8, LANES), 0)
    blocks = freqs // LANES

    def part(index, _):
        g = index // blocks
        block = index % blocks
        lanes = pl.ds(pl.multiple_of(block * LANES, LANES), LANES)
        sines = pl.ds(pl.multiple_of(freqs + block * LANES, LANES), LANES)

        @pl.when(block == 0)
        def _():
            fetch(g).wait()

        def pair(k):
            sums = site_sums(tiles, wide, [g * 8 + k, g * 8 + k + 4], range(REALS), block, lanes)
            return [
                [merge(sums[0, b][c], sums[1, b][c], 4, place) for c in range(2)]
                for b in range(REALS)
            ]

        def both(k):
            first = pair(k)
            second = pair(k + 2)
            return [
                [merge(first[b][c], second[b][c], 2, place) for c in range(2)]
                for b in range(REALS)
            ]

        first = both(0)
        second = both(1)
        for b in range(REALS):
            at = pl.ds(pl.multiple_of(b * sens + g * 8, 8), 8)
            rows[at, lanes] = merge(first[b][0], second[b][0], 1, place)
            rows[at, sines] = merge(first[b][1], second[b][1], 1, place)
        return 0

    lax.fori_loop(0, (sens // 8) * blocks, part, 0)
    half = REALS * sens // 2
    series = synthesize(rows, high, low, energy + energy, 8)
    row = lax.broadcasted_iota(jnp.int32, (half, freqs), 0)
    lane = lane_of((half, freqs))
    carried = series[:half, freqs - 1 :]
    full[:half, :] = series[:half]
    full[half:, :] = jnp.where(lane == freqs - 1, carried, series[half:])
    mine[...] = full[pl.ds(pl.multiple_of(core[0] * half, 8), half), :]
    other[...] = full[pl.ds(pl.multiple_of((1 - core[0]) * half, 8), half), :]


def site_kernel(weighted, prior, tiles, high, low, out, wide, rows):
    freqs = tiles.shape[3]
    energy = widen(weighted, prior, wide)
    place = lax.broadcasted_iota(jnp.int32, (8, LANES), 0)

    def part(block, _):
        lanes = pl.ds(pl.multiple_of(block * LANES, LANES), LANES)
        sines = pl.ds(pl.multiple_of(freqs + block * LANES, LANES), LANES)
        for low_b in range(0, REALS, 2):
            sums = site_sums(tiles, wide, range(4), (low_b, low_b + 1), block, lanes)
            for c, where in ((0, lanes), (1, sines)):
                blocks = [sums[j, low_b + b][c] for b in range(2) for j in range(4)]
                for width in (4, 2, 1):
                    half = len(blocks) // 2
                    blocks = [
                        merge(x, y, width, place) for x, y in zip(blocks[:half], blocks[half:])
                    ]
                rows[pl.ds(low_b * 4, 8), where] = blocks[0]
        return 0

    lax.fori_loop(0, freqs // LANES, part, 0)
    out[...] = synthesize(rows, high, low, energy, REALS)


def spread_kernel(mine, got, out, *, stride, begin):
    values = mine[...] + got[...]
    count, freqs = values.shape
    row = lax.broadcasted_iota(jnp.int32, (count, freqs), 0) - begin
    carried = lane_of((count, freqs)) == freqs - 1
    _, second, third = three(values)
    second_row = (row >= stride) & (row < 2 * stride)
    third_row = (row >= 2 * stride) & (row < 3 * stride)
    values = jnp.where(carried & second_row, second, values)
    values = jnp.where(carried & third_row, third, values)
    block = values.astype(BF16)
    for k in range(out.shape[0]):
        out[k] = block


def sum_kernel(got, out):
    total = got[0].astype(F32)
    for k in range(1, got.shape[0]):
        total = total + got[k].astype(F32)
    out[...] = total


def last_kernel(got, begin, later, alpha, series, residual, estimate, predicted):
    reals, sens, steps = estimate.shape
    sites = predicted.shape[1]
    count = reals * sites
    total = got[0].astype(F32)
    for k in range(1, got.shape[0]):
        total = total + got[k].astype(F32)
    last = total.shape[1] - 1
    for b in range(reals):
        rows = [count + k * reals + b for k in range(3)]
        energy = sum(total[r : r + 1, last:] for r in rows)

        def value(ref, kind):
            return ref[0:1, kind * reals + b : kind * reals + b + 1]

        beta = value(later, 0) / value(begin, 0)
        curve = energy + value(later, 1) + 2.0 * beta * value(later, 2)
        curve = curve + beta * beta * value(begin, 1)
        first = value(alpha, 0)
        second = value(later, 0) / curve
        at = slice(b * sens, (b + 1) * sens)
        values = series[at, :]
        result = first * values + second * (residual[at, :] + beta * values)
        estimate[b] = result[:, :steps]
        low = total[b * sites : (b + 1) * sites]
        high = total[count + b * sites : count + (b + 1) * sites]
        predicted[b] = (first * low + second * high)[:, :steps]


def in_hbm(array):
    return pltpu.with_memory_space_constraint(array, pltpu.HBM)


def call(kernel, name, outs, scratch, specs, *args, semaphores=(), limit=24 * 2**20):
    scratch = [pltpu.VMEM(*one) for one in scratch]
    args = [in_hbm(arg) if spec is HBM else arg for arg, spec in zip(args, specs)]
    scratch += [pltpu.SemaphoreType.DMA((number,)) for number in semaphores]
    return pl.pallas_call(
        kernel,
        in_specs=specs,
        out_specs=[VMEM] * len(outs),
        out_shape=[jax.ShapeDtypeStruct(*out) for out in outs],
        scratch_shapes=scratch,
        compiler_params=pltpu.CompilerParams(vmem_limit_bytes=limit),
        name=name,
    )(*args)


def on_device(records, tiles, gauges, prior, noise):
    reals, sensors, steps = records.shape
    points, freqs = prior.shape
    sites = gauges.shape[1]
    tables = make_tables(freqs)
    senders = lax.axis_size("y") * lax.axis_size("x")
    heights = lax.axis_size("z")
    place = lax.axis_index("y") * lax.axis_size("x") + lax.axis_index("x")
    core = lax.axis_index("core").astype(jnp.int32).reshape(1)
    start = (place // (2 * reals) * BAND).astype(jnp.int32).reshape(1)
    pick = lax.rem(place, reals).astype(jnp.int32).reshape(1)
    core, pick, start, prior, gauges, records = lax.optimization_barrier(
        (core, pick, start, prior, gauges, records)
    )
    count = reals * sensors
    half = count // 2
    block_rows = BAND * freqs // LANES
    message = ((senders, block_rows + EXTRA, LANES), BF16)
    weighted_shape = (senders, block_rows, LANES)
    wide_shape = (3 * senders // 2, block_rows, LANES)
    spectra = ((count // 8, 8, 2 * freqs), F32)
    flat = ((count, 2 * freqs), F32)
    rows = ((count, freqs), F32)
    tile = ((8, LANES), F32)

    def swap(block):
        return lax.ppermute(block, "core", [(0, 1), (1, 0)])

    def site(weighted, name, tables):
        return call(
            site_kernel,
            name,
            [((reals * sites, freqs), F32)],
            [(wide_shape, F32), ((reals * sites, 2 * freqs), F32)],
            [VMEM] * 5,
            *(weighted, prior, gauges, *tables),
        )[0]

    bands = points // BAND
    pieces = bands * (sensors // 8)
    local = (tiles.shape, BF16)
    sent, series, noisy, *tables = call(
        first_kernel,
        "first",
        [message, rows, ((sensors, 1), F32)] + [(table.shape, BF16) for table in tables],
        [(records.shape, F32), ((1, sensors), F32), local, spectra],
        [HBM] * 5,
        *(records, noise.reshape(1, sensors), tiles, *tables),
        semaphores=[4 + pieces],
    )
    got = lax.all_to_all(sent, SENS, 0, 0)
    sent, points_0, begin = call(
        weigh_kernel,
        "weigh",
        [(weighted_shape, BF16), ((block_rows, LANES), F32), tile],
        [],
        [VMEM, VMEM, SMEM],
        *(got, prior, start),
    )
    weighted_0 = lax.all_to_all(sent, SENS, 0, 0)
    mine, other = call(
        forward_kernel,
        "forward",
        [((half, freqs), F32)] * 2,
        [(wide_shape, F32), flat, rows, local],
        [SMEM, VMEM, VMEM, HBM, VMEM, VMEM],
        *(core, weighted_0, prior, tiles, *tables),
        semaphores=[sensors // 8],
    )
    (sent,) = call(
        functools.partial(spread_kernel, stride=8, begin=0),
        "spread",
        [((heights, half, freqs), BF16)],
        [],
        [VMEM] * 2,
        *(mine, swap(other)),
    )
    got = lax.all_to_all(sent, "z", 0, 0)
    (mine,) = call(sum_kernel, "gather", [((half, freqs), F32)], [], [VMEM], got)
    weighted_0, mine = lax.optimization_barrier((weighted_0, mine))
    site_0 = site(weighted_0, "site_0", tables)
    theirs, site_0 = lax.optimization_barrier((swap(mine), site_0))
    sent, residual, alpha = call(
        second_kernel,
        "second",
        [message, rows, tile],
        [rows, local, spectra],
        [SMEM] + [VMEM] * 5 + [HBM, VMEM, VMEM],
        *(core, mine, theirs, series, noisy, begin, tiles, *tables),
        semaphores=[pieces],
    )
    got = lax.all_to_all(sent, SENS, 0, 0)
    sent, later = call(
        weigh_next_kernel,
        "weigh_next",
        [(weighted_shape, BF16), tile],
        [],
        [VMEM] * 4 + [SMEM] * 2,
        *(got, prior, points_0, begin, pick, start),
    )
    weighted_1 = lax.all_to_all(sent, SENS, 0, 0)

    block = jnp.concatenate([site_0, site(weighted_1, "site_1", tables)])
    (sent,) = call(
        functools.partial(spread_kernel, stride=reals, begin=reals * sites),
        "spread_sites",
        [((heights,) + block.shape, BF16)],
        [],
        [VMEM] * 2,
        *(block, swap(block)),
    )
    got = lax.all_to_all(sent, "z", 0, 0)
    estimate, predicted = call(
        last_kernel,
        "last",
        [((reals, sensors, steps), F32), ((reals, sites, steps), F32)],
        [],
        [VMEM] * 6,
        *(got, begin, later, alpha, series, residual),
    )
    return (estimate, predicted)


def solution(mesh):
    fine = Mesh(mesh.devices.reshape(4, 4, 8, 2), SENS + PTS)
    return jax.shard_map(
        on_device,
        mesh=fine,
        in_specs=(
            P(None, SENS, None),
            P(None, SENS, PTS, None),
            P(None, SENS, PTS, None),
            P(PTS, None),
            P(SENS),
        ),
        out_specs=(P(None, SENS, None), P(None, SENS, None)),
        check_vma=False,
    )
```

```python
import functools

import jax
import jax.numpy as jnp
import numpy as np
from jax import lax
from jax.experimental import pallas as pl
from jax.experimental.pallas import tpu as pltpu
from jax.sharding import Mesh
from jax.sharding import PartitionSpec as P

SENS = ("y", "x")
PTS = ("z", "core")
REALS = 4
LANES = 128
BAND = 32
EXTRA = 8
F32 = jnp.float32
BF16 = jnp.bfloat16
VMEM = pl.BlockSpec(memory_space=pltpu.VMEM)
HBM = pl.BlockSpec(memory_space=pltpu.HBM)
SMEM = pl.BlockSpec(memory_space=pltpu.SMEM)


def make_tables(freqs):
    padded = 2 * (freqs - 1)
    steps = np.arange(freqs, dtype=np.int64)
    angle = (steps[:, None] * steps[None, :] % padded) * (2.0 * np.pi / padded)
    both = np.concatenate([np.cos(angle), -np.sin(angle)], axis=1)
    high = both.astype(BF16)
    low = (both - high.astype(np.float64)).astype(BF16)
    return jnp.asarray(high), jnp.asarray(low)


def frequency_weights(freqs):
    at = lax.broadcasted_iota(jnp.int32, (1, 2 * freqs), 1)
    at = jnp.where(at < freqs, at, at - freqs)
    padded = 2 * (freqs - 1)
    return jnp.where((at == 0) | (at == freqs - 1), 1.0 / padded, 2.0 / padded)


def product(left, high, low, ready=None):
    rows = left.shape[0]
    first = left.astype(BF16)
    second = (left - first.astype(F32)).astype(BF16)

    def dot(a, b):
        return jnp.dot(a, b, preferred_element_type=F32)

    both = dot(jnp.concatenate([first, second]), high[...])
    if ready is not None:
        ready()
    return both[:rows] + (dot(first, low[...]) + both[rows:])


def lane_of(shape):
    return lax.broadcasted_iota(jnp.int32, shape, len(shape) - 1)


def three(values):
    first = values.astype(BF16).astype(F32)
    rest = values - first
    second = rest.astype(BF16).astype(F32)
    return first, second, rest - second


def write_scalars(out, columns):
    lane = lane_of((8, LANES))
    tile = jnp.zeros((8, LANES), F32)
    for k, column in enumerate(columns):
        tile = jnp.where(lane == k, column, tile)
    first, second, third = three(tile)
    tile = first + pltpu.roll(second, 32, 1) + pltpu.roll(third, 64, 1)
    block = tile.astype(BF16)
    rows = out.shape[1] - EXTRA
    for k in range(out.shape[0]):
        out[k, rows:, :] = block


def band_sum(first, second, start, count):
    total = jnp.zeros((8, first.shape[1]), F32)
    for row in range(start, start + count, 8):
        total = total + first[row : row + 8, :] * second[row : row + 8, :]
    return jnp.sum(total, axis=1, keepdims=True)


def pieces_of(source, target, done, first=0):
    groups = source.shape[1] // 8

    def copy(band, group):
        at = (slice(None), pl.ds(group * 8, 8), pl.ds(pl.multiple_of(band * BAND, BAND), BAND))
        return pltpu.make_async_copy(
            source.at[at], target.at[at], done.at[first + band * groups + group]
        )

    copies = [copy(b, g) for b in range(source.shape[2] // BAND) for g in range(groups)]
    return copy, copies


def groups_of(source, target, done):
    def copy(group):
        at = pl.ds(group * 8, 8)
        return pltpu.make_async_copy(source.at[:, at], target.at[:, at], done.at[group])

    return copy


def send_points(series, tiles, copy, high, low, spec, out, ready=None):
    sens, points, freqs = tiles.shape[1:]
    pair = product(series[...], high, low, ready) * frequency_weights(freqs)
    spec[...] = pair.reshape(spec.shape)
    blocks = freqs // LANES

    def part(index, _):
        band = index // blocks
        block = index % blocks
        lanes = pl.ds(pl.multiple_of(block * LANES, LANES), LANES)
        sines = pl.ds(pl.multiple_of(freqs + block * LANES, LANES), LANES)
        range_ = pl.ds(pl.multiple_of(band * BAND, BAND), BAND)

        def group(g, acc):
            @pl.when(block == 0)
            def _():
                copy(band, g).wait()

            acc = list(acc)
            rows = [b * (sens // 8) + g for b in range(REALS)]
            for j in range(8):
                tr = tiles[0, g * 8 + j, range_, lanes].astype(F32)
                ti = tiles[1, g * 8 + j, range_, lanes].astype(F32)
                for b in range(REALS):
                    sr = spec[rows[b], j : j + 1, lanes]
                    si = spec[rows[b], j : j + 1, sines]
                    re, im = acc[b]
                    acc[b] = (re + (sr * tr + si * ti), im + (si * tr - sr * ti))
            return tuple(acc)

        zero = jnp.zeros((BAND, LANES), F32)
        acc = lax.fori_loop(0, sens // 8, group, ((zero, zero),) * REALS)
        rows = pl.ds(pl.multiple_of(block * BAND, BAND), BAND)
        for b in range(REALS):
            for c in range(2):
                out[band * 2 * REALS + c * REALS + b, rows, :] = acc[b][c].astype(BF16)
        return 0

    lax.fori_loop(0, (points // BAND) * blocks, part, 0)


def first_kernel(
    records, noise, tiles_in, high_in, low_in, out, series, column, high, low, head, raw, raw_noise, tiles, spec, done
):
    reals, sens, steps = records.shape
    moves = (
        (records, raw),
        (noise, raw_noise),
        (high_in, high),
        (low_in, low),
        (tiles_in.at[:, :8], head),
    )
    copies = [pltpu.make_async_copy(*move, done.at[k]) for k, move in enumerate(moves)]
    fetch, pieces = pieces_of(tiles_in, tiles, done, len(copies))
    for copy in copies[:4] + pieces + copies[4:]:
        copy.start()
    copies[0].wait()
    copies[1].wait()
    row = lax.broadcasted_iota(jnp.int32, (sens, sens), 0)
    noises = jnp.where(row == lane_of((sens, sens)), raw_noise[...], 0.0)
    noises = jnp.sum(noises, axis=1, keepdims=True)
    column[...] = noises
    series[...] = jnp.zeros_like(series)
    columns = [[], []]
    for b in range(reals):
        series[b * sens : (b + 1) * sens, :steps] = raw[b]
    for b in range(reals):
        values = series[b * sens : (b + 1) * sens, :]
        columns[0].append(band_sum(values, values, 0, sens))
        columns[1].append(band_sum(values, values * noises, 0, sens))
    write_scalars(out, columns[0] + columns[1])
    copies[2].wait()
    send_points(series, tiles, fetch, high, low, spec, out, copies[3].wait)
    copies[4].wait()


def second_kernel(
    core, mine, theirs, series, noise, begin, tiles_in, high, low, out, residual, alpha, image, tiles, spec, done
):
    fetch, pieces = pieces_of(tiles_in, tiles, done)
    for copy in pieces:
        copy.start()
    half, freqs = mine.shape
    sens = 2 * half // REALS
    image[pl.ds(pl.multiple_of(core[0] * half, 8), half), :] = mine[...]
    image[pl.ds(pl.multiple_of((1 - core[0]) * half, 8), half), :] = theirs[...]
    lane = lane_of((8, LANES))
    tile = jnp.zeros((8, LANES), F32)
    real = lane_of((sens, freqs)) < freqs - 1
    last = freqs - 1
    columns = [[], [], []]
    for b in range(REALS):
        energy = image[b : b + 1, last:] + image[8 + b : 9 + b, last:] + image[16 + b : 17 + b, last:]
        scale = begin[0:1, b : b + 1] / (energy + begin[0:1, REALS + b : REALS + b + 1])
        tile = jnp.where(lane == b, scale, tile)
        rows = slice(b * sens, (b + 1) * sens)
        values = series[rows, :]
        noisy = noise[...]
        left = values - scale * (jnp.where(real, image[rows, :], 0.0) + noisy * values)
        residual[rows, :] = left
        columns[0].append(band_sum(left, left, 0, sens))
        columns[1].append(band_sum(left, left * noisy, 0, sens))
        columns[2].append(band_sum(left, values * noisy, 0, sens))
    alpha[...] = tile
    write_scalars(out, columns[0] + columns[1] + columns[2])
    send_points(residual, tiles, fetch, high, low, spec, out)


def sum_message(got):
    rows = got.shape[1] - EXTRA
    total = got[0, :rows, :].astype(F32)
    extra = got[0, rows:, :].astype(F32)
    for k in range(1, got.shape[0]):
        total = total + got[k, :rows, :].astype(F32)
        extra = extra + got[k, rows:, :].astype(F32)
    sums = jnp.broadcast_to(jnp.sum(extra, axis=0, keepdims=True), (8, LANES))
    sums = sums + pltpu.roll(sums, LANES - 32, 1) + pltpu.roll(sums, LANES - 64, 1)
    return total, sums


def put_weighted(total, prior, start, out):
    points = pl.ds(pl.multiple_of(start[0], BAND), BAND)
    for block in range(prior.shape[1] // LANES):
        rows = slice(block * BAND, (block + 1) * BAND)
        lanes = slice(block * LANES, (block + 1) * LANES)
        part = (total[rows] * prior[points, lanes]).astype(BF16)
        for k in range(out.shape[0]):
            out[k, rows, :] = part


def weigh_kernel(got, prior, start, out, kept, sums_out):
    total, sums = sum_message(got)
    kept[...] = total
    sums_out[...] = sums
    put_weighted(total, prior, start, out)


def weigh_next_kernel(got, prior, before, begin, pick, start, out, sums_out):
    total, sums = sum_message(got)
    sums_out[...] = sums
    lane = lane_of((8, LANES))
    ratio = sums / jnp.where(lane < REALS, begin[...], 1.0)
    beta = jnp.sum(jnp.where(lane == pick[0], ratio, 0.0), axis=1, keepdims=True)[0:1]
    put_weighted(total + beta * before[...], prior, start, out)


def widen(weighted, prior, wide):
    energy = [jnp.zeros((8, LANES), F32)] * REALS
    parts = weighted.shape[0] // (2 * REALS)
    for h in range(parts):
        for block in range(prior.shape[1] // LANES):
            for row in range(0, BAND, 16):
                lanes = slice(block * LANES, (block + 1) * LANES)
                inverse = 1.0 / prior[h * BAND + row : h * BAND + row + 16, lanes]
                for b in range(REALS):
                    at = slice(block * BAND + row, block * BAND + row + 16)
                    re = weighted[h * 2 * REALS + b, at, :].astype(F32)
                    im = weighted[h * 2 * REALS + REALS + b, at, :].astype(F32)
                    wide[b * parts + h, at, :] = re
                    wide[(REALS + b) * parts + h, at, :] = im
                    wide[(2 * REALS + b) * parts + h, at, :] = re + im
                    term = (re * re + im * im) * inverse
                    energy[b] = energy[b] + (term[:8] + term[8:])
    return [
        jnp.sum(jnp.sum(e, axis=0, keepdims=True), axis=1, keepdims=True) for e in energy
    ]


def merge(first, second, width, place):
    low = (place & width) == 0
    other = jnp.where(low, second, first)
    if width == 4:
        other = pltpu.roll(other, 4, 0)
    else:
        other = jnp.where(low, pltpu.roll(other, 8 - width, 0), pltpu.roll(other, width, 0))
    return jnp.where(low, first, second) + other


def site_sums(tiles, wide, sites, reals, block, lanes):
    sums = {}
    parts = tiles.shape[2] // BAND
    for p in range(0, tiles.shape[2], 16):
        h, row = divmod(p, BAND)
        terms = []
        for s in sites:
            tr, ti = (tiles[c, s, pl.ds(p, 16), lanes].astype(F32) for c in range(2))
            terms.append((tr, ti, tr + ti))
        for q in (0, 8):
            at = pl.ds(pl.multiple_of(block * BAND + row + q, 8), 8)
            for b in reals:
                values = [wide[(c * REALS + b) * parts + h, at, :] for c in range(3)]
                for j in range(len(sites)):
                    new = [values[c] * terms[j][c][q : q + 8] for c in range(3)]
                    if (j, b) in sums:
                        new = [x + y for x, y in zip(sums[j, b], new)]
                    sums[j, b] = new
    return {k: (x - y, z - x - y) for k, (x, y, z) in sums.items()}


def synthesize(rows, high, low, energy, stride):
    count, freqs = rows.shape[0], rows.shape[1] // 2
    scaled = rows[...] * frequency_weights(freqs)
    series = product(scaled[:, :freqs], high.at[:, :freqs], low.at[:, :freqs]) + product(
        scaled[:, freqs:], high.at[:, freqs:], low.at[:, freqs:]
    )
    row = lax.broadcasted_iota(jnp.int32, (count, freqs), 0)
    lane = lane_of((count, freqs))
    carried = jnp.zeros((count, 1), F32)
    index = row[:, 0:1]
    for b in range(REALS):
        hit = (index % stride == b) & (index < 3 * stride)
        carried = jnp.where(hit, energy[b], carried)
    return jnp.where(lane == freqs - 1, carried, series)


def forward_kernel(
    core, weighted, prior, head, tiles_in, high, low, mine, other, wide, rows, full, tiles, done
):
    sens, points, freqs = tiles.shape[1:]
    fetch = groups_of(tiles_in, tiles, done)
    for k in range(1, sens // 8):
        fetch(k).start()
    energy = widen(weighted, prior, wide)
    place = lax.broadcasted_iota(jnp.int32, (8, LANES), 0)
    blocks = freqs // LANES

    def part(index, source, begin):
        g = index // blocks
        block = index % blocks
        lanes = pl.ds(pl.multiple_of(block * LANES, LANES), LANES)
        sines = pl.ds(pl.multiple_of(freqs + block * LANES, LANES), LANES)
        base = begin * 8

        def pair(k):
            sensors = [base + k, base + k + 4]
            sums = site_sums(source, wide, sensors, range(REALS), block, lanes)
            return [
                [merge(sums[0, b][c], sums[1, b][c], 4, place) for c in range(2)]
                for b in range(REALS)
            ]

        def both(k):
            first = pair(k)
            second = pair(k + 2)
            return [
                [merge(first[b][c], second[b][c], 2, place) for c in range(2)]
                for b in range(REALS)
            ]

        first = both(0)
        second = both(1)
        for b in range(REALS):
            at = pl.ds(pl.multiple_of(b * sens + g * 8, 8), 8)
            rows[at, lanes] = merge(first[b][0], second[b][0], 1, place)
            rows[at, sines] = merge(first[b][1], second[b][1], 1, place)
        return 0

    def head_part(index, _):
        return part(index, head, 0)

    def tile_part(index, _):
        group = index // blocks

        @pl.when(index % blocks == 0)
        def _():
            fetch(group).wait()

        return part(index, tiles, group)

    lax.fori_loop(0, blocks, head_part, 0)
    lax.fori_loop(blocks, (sens // 8) * blocks, tile_part, 0)
    half = REALS * sens // 2
    series = synthesize(rows, high, low, energy + energy, 8)
    row = lax.broadcasted_iota(jnp.int32, (half, freqs), 0)
    lane = lane_of((half, freqs))
    carried = series[:half, freqs - 1 :]
    full[:half, :] = series[:half]
    full[half:, :] = jnp.where(lane == freqs - 1, carried, series[half:])
    mine[...] = full[pl.ds(pl.multiple_of(core[0] * half, 8), half), :]
    other[...] = full[pl.ds(pl.multiple_of((1 - core[0]) * half, 8), half), :]


def site_kernel(weighted, prior, tiles, high, low, out, wide, rows):
    freqs = tiles.shape[3]
    energy = widen(weighted, prior, wide)
    place = lax.broadcasted_iota(jnp.int32, (8, LANES), 0)

    def part(block, _):
        lanes = pl.ds(pl.multiple_of(block * LANES, LANES), LANES)
        sines = pl.ds(pl.multiple_of(freqs + block * LANES, LANES), LANES)
        for low_b in range(0, REALS, 2):
            sums = site_sums(tiles, wide, range(4), (low_b, low_b + 1), block, lanes)
            for c, where in ((0, lanes), (1, sines)):
                blocks = [sums[j, low_b + b][c] for b in range(2) for j in range(4)]
                for width in (4, 2, 1):
                    half = len(blocks) // 2
                    blocks = [
                        merge(x, y, width, place) for x, y in zip(blocks[:half], blocks[half:])
                    ]
                rows[pl.ds(low_b * 4, 8), where] = blocks[0]
        return 0

    lax.fori_loop(0, freqs // LANES, part, 0)
    out[...] = synthesize(rows, high, low, energy, REALS)


def spread_kernel(mine, got, out, *, stride, begin):
    values = mine[...] + got[...]
    count, freqs = values.shape
    row = lax.broadcasted_iota(jnp.int32, (count, freqs), 0) - begin
    carried = lane_of((count, freqs)) == freqs - 1
    _, second, third = three(values)
    second_row = (row >= stride) & (row < 2 * stride)
    third_row = (row >= 2 * stride) & (row < 3 * stride)
    values = jnp.where(carried & second_row, second, values)
    values = jnp.where(carried & third_row, third, values)
    block = values.astype(BF16)
    for k in range(out.shape[0]):
        out[k] = block


def sum_kernel(got, out):
    total = got[0].astype(F32)
    for k in range(1, got.shape[0]):
        total = total + got[k].astype(F32)
    out[...] = total


def last_kernel(got, begin, later, alpha, series, residual, estimate, predicted):
    reals, sens, steps = estimate.shape
    sites = predicted.shape[1]
    count = reals * sites
    total = got[0].astype(F32)
    for k in range(1, got.shape[0]):
        total = total + got[k].astype(F32)
    last = total.shape[1] - 1
    for b in range(reals):
        rows = [count + k * reals + b for k in range(3)]
        energy = sum(total[r : r + 1, last:] for r in rows)

        def value(ref, kind):
            return ref[0:1, kind * reals + b : kind * reals + b + 1]

        beta = value(later, 0) / value(begin, 0)
        curve = energy + value(later, 1) + 2.0 * beta * value(later, 2)
        curve = curve + beta * beta * value(begin, 1)
        first = value(alpha, 0)
        second = value(later, 0) / curve
        at = slice(b * sens, (b + 1) * sens)
        values = series[at, :]
        result = first * values + second * (residual[at, :] + beta * values)
        estimate[b] = result[:, :steps]
        low = total[b * sites : (b + 1) * sites]
        high = total[count + b * sites : count + (b + 1) * sites]
        predicted[b] = (first * low + second * high)[:, :steps]


def in_hbm(array):
    return pltpu.with_memory_space_constraint(array, pltpu.HBM)


def call(kernel, name, outs, scratch, specs, *args, semaphores=(), limit=24 * 2**20):
    scratch = [pltpu.VMEM(*one) for one in scratch]
    args = [in_hbm(arg) if spec is HBM else arg for arg, spec in zip(args, specs)]
    scratch += [pltpu.SemaphoreType.DMA((number,)) for number in semaphores]
    return pl.pallas_call(
        kernel,
        in_specs=specs,
        out_specs=[VMEM] * len(outs),
        out_shape=[jax.ShapeDtypeStruct(*out) for out in outs],
        scratch_shapes=scratch,
        compiler_params=pltpu.CompilerParams(vmem_limit_bytes=limit),
        name=name,
    )(*args)


def on_device(records, tiles, gauges, prior, noise):
    reals, sensors, steps = records.shape
    points, freqs = prior.shape
    sites = gauges.shape[1]
    tables = make_tables(freqs)
    senders = lax.axis_size("y") * lax.axis_size("x")
    heights = lax.axis_size("z")
    place = lax.axis_index("y") * lax.axis_size("x") + lax.axis_index("x")
    core = lax.axis_index("core").astype(jnp.int32).reshape(1)
    start = (place // (2 * reals) * BAND).astype(jnp.int32).reshape(1)
    pick = lax.rem(place, reals).astype(jnp.int32).reshape(1)
    core, pick, start, prior, gauges, records = lax.optimization_barrier(
        (core, pick, start, prior, gauges, records)
    )
    count = reals * sensors
    half = count // 2
    block_rows = BAND * freqs // LANES
    message = ((senders, block_rows + EXTRA, LANES), BF16)
    weighted_shape = (senders, block_rows, LANES)
    wide_shape = (3 * senders // 2, block_rows, LANES)
    spectra = ((count // 8, 8, 2 * freqs), F32)
    flat = ((count, 2 * freqs), F32)
    rows = ((count, freqs), F32)
    tile = ((8, LANES), F32)

    def swap(block):
        return lax.ppermute(block, "core", [(0, 1), (1, 0)])

    def site(weighted, name, tables):
        return call(
            site_kernel,
            name,
            [((reals * sites, freqs), F32)],
            [(wide_shape, F32), ((reals * sites, 2 * freqs), F32)],
            [VMEM] * 5,
            *(weighted, prior, gauges, *tables),
        )[0]

    bands = points // BAND
    pieces = bands * (sensors // 8)
    local = (tiles.shape, BF16)
    sent, series, noisy, *tables, head = call(
        first_kernel,
        "first",
        [message, rows, ((sensors, 1), F32)]
        + [(table.shape, BF16) for table in tables]
        + [((2, 8, points, freqs), BF16)],
        [(records.shape, F32), ((1, sensors), F32), local, spectra],
        [HBM] * 5,
        *(records, noise.reshape(1, sensors), tiles, *tables),
        semaphores=[5 + pieces],
    )
    got = lax.all_to_all(sent, SENS, 0, 0)
    sent, points_0, begin = call(
        weigh_kernel,
        "weigh",
        [(weighted_shape, BF16), ((block_rows, LANES), F32), tile],
        [],
        [VMEM, VMEM, SMEM],
        *(got, prior, start),
    )
    weighted_0 = lax.all_to_all(sent, SENS, 0, 0)
    mine, other = call(
        forward_kernel,
        "forward",
        [((half, freqs), F32)] * 2,
        [(wide_shape, F32), flat, rows, local],
        [SMEM, VMEM, VMEM, VMEM, HBM, VMEM, VMEM],
        *(core, weighted_0, prior, head, tiles, *tables),
        semaphores=[sensors // 8],
    )
    (sent,) = call(
        functools.partial(spread_kernel, stride=8, begin=0),
        "spread",
        [((heights, half, freqs), BF16)],
        [],
        [VMEM] * 2,
        *(mine, swap(other)),
    )
    got = lax.all_to_all(sent, "z", 0, 0)
    (mine,) = call(sum_kernel, "gather", [((half, freqs), F32)], [], [VMEM], got)
    weighted_0, mine = lax.optimization_barrier((weighted_0, mine))
    site_0 = site(weighted_0, "site_0", tables)
    theirs, site_0 = lax.optimization_barrier((swap(mine), site_0))
    sent, residual, alpha = call(
        second_kernel,
        "second",
        [message, rows, tile],
        [rows, local, spectra],
        [SMEM] + [VMEM] * 5 + [HBM, VMEM, VMEM],
        *(core, mine, theirs, series, noisy, begin, tiles, *tables),
        semaphores=[pieces],
    )
    got = lax.all_to_all(sent, SENS, 0, 0)
    sent, later = call(
        weigh_next_kernel,
        "weigh_next",
        [(weighted_shape, BF16), tile],
        [],
        [VMEM] * 4 + [SMEM] * 2,
        *(got, prior, points_0, begin, pick, start),
    )
    weighted_1 = lax.all_to_all(sent, SENS, 0, 0)

    block = jnp.concatenate([site_0, site(weighted_1, "site_1", tables)])
    (sent,) = call(
        functools.partial(spread_kernel, stride=reals, begin=reals * sites),
        "spread_sites",
        [((heights,) + block.shape, BF16)],
        [],
        [VMEM] * 2,
        *(block, swap(block)),
    )
    got = lax.all_to_all(sent, "z", 0, 0)
    estimate, predicted = call(
        last_kernel,
        "last",
        [((reals, sensors, steps), F32), ((reals, sites, steps), F32)],
        [],
        [VMEM] * 6,
        *(got, begin, later, alpha, series, residual),
    )
    return (estimate, predicted)


def solution(mesh):
    fine = Mesh(mesh.devices.reshape(4, 4, 8, 2), SENS + PTS)
    return jax.shard_map(
        on_device,
        mesh=fine,
        in_specs=(
            P(None, SENS, None),
            P(None, SENS, PTS, None),
            P(None, SENS, PTS, None),
            P(PTS, None),
            P(SENS),
        ),
        out_specs=(P(None, SENS, None), P(None, SENS, None)),
        check_vma=False,
    )
```
